32 devices in a mesh: dp: 2 (over x), expert: 16 (over z, y, core).
Axes of the slice: x: 2, y: 2, z: 4, core: 2. Of those that a mesh axis runs over, the one named last changes fastest.
Arguments:
- tokens: bfloat16 [2048, 4096], P('expert', 'dp'), may hold values from -6 to 6
- expert_ids: int32 [2048, 8], P('expert'), may hold values from 0 to 15, all different within a row; in each aligned block of 128 rows (0 to 127, 128 to 255, ...) at most 96 rows name the same one
- gates: float32 [2048, 8], P('expert'), may hold values from 0.1 to 0.6
- cotangent: bfloat16 [2048, 4096], P('expert', 'dp'), may hold values from -0.59765625 to 0.59765625
- partner: int32 [16], replicated, may hold values from -1 to 15, as said below
- w_gate: bfloat16 [16, 4096, 1024], P('expert', 'dp'), may hold values from -0.09375 to 0.09375
- w_up: bfloat16 [16, 4096, 1024], P('expert', 'dp'), may hold values from -0.09375 to 0.09375
- w_down: bfloat16 [16, 1024, 4096], P('expert', None, 'dp'), may hold values from -0.1875 to 0.1875
Outputs:
- mixed: bfloat16 [2048, 4096], P('expert', 'dp')
- grad_tokens: bfloat16 [2048, 4096], P('expert', 'dp')
- grad_gates: float32 [2048, 8], P('expert')
- grad_gate_w: bfloat16 [16, 4096, 1024], P('expert', 'dp')
- grad_up_w: bfloat16 [16, 4096, 1024], P('expert', 'dp')
- grad_down_w: bfloat16 [16, 1024, 4096], P('expert', None, 'dp')
The draws below stay inside these ranges and needn't reach their ends.
Inputs may be any that keep to these rules, and one draw needn't show every extreme that they name: `expert_ids`: each row names 8 different experts. In each aligned block of 128 rows no expert is named more than 64 + 32 times, and in some block some expert is named exactly that many times. Exactly 8 entries are -1. The others name distinct experts, and for each such expert e, partner[e] is -1.
All inputs are finite; a program needn't handle non-finite values.
Results may differ from the reference program's by a relative error of at most 0.023.
Values may be sent and summed in bfloat16 or wider, within the bound.
A program may use at most 192 MiB of HBM per device.

```python
import math
import jax
import jax.numpy as jnp
import numpy as np
from jax import lax

D = 4096
H = 1024
K = 8
TOK_DEV = 128
EXPERTS = 16
TOKENS = 2048
CAP = 64
SPILL = 32
N_DP = 2
N_EXPERT = 16


def draw_partner(key, part):
    order = jax.random.permutation(key, N_EXPERT).astype(jnp.int32)
    last = N_EXPERT - 1
    where_last = jnp.argmax((order == last).astype(jnp.int32)).astype(jnp.int32)
    first = order[0]
    order = order.at[where_last].set(first).at[0].set(last)
    half = N_EXPERT // 2
    return jnp.full((N_EXPERT,), -1, jnp.int32).at[order[half:]].set(order[:half])


def steps_of(rng, extent, shards, smallest, largest):
    def one(dim, parts):
        steps = jax.random.uniform(jax.random.fold_in(jax.random.fold_in(rng, 6), dim), (parts,), jnp.float32, smallest / len(shards), largest / len(shards))
        return jnp.repeat(jnp.exp(steps), extent[dim] // parts).reshape((-1,) + (1,) * (len(extent) - dim - 1))

    level = one(*shards[0])
    for cut in shards[1:]:
        level = level * one(*cut)
    return level


def deal_out(stream_key, own, number, rows, count, top, bound, slope):
    order = jax.random.permutation(stream_key, count)
    packed, common = portions_of(count, rows * top, bound, slope, True), portions_of(count, rows * top, bound, slope, False)
    places = jnp.arange(count)

    def named(sizes, rotation):
        used = int((sizes > 0).sum())
        fixed = max(1, used // 4)
        passed = fixed + (places - fixed + rotation * (used - fixed)) % max(1, count - fixed)
        return jnp.zeros((count,), jnp.int32).at[order[jnp.where(places < fixed, places, passed)]].set(jnp.asarray(sizes, jnp.int32))

    sizes = jnp.where(number % 4 == 0, named(packed, number // 4), named(common, number - number // 4 - 1))
    mixed = jax.random.permutation(jax.random.fold_in(own, 3), count)
    donor, taker = mixed[0:count // 2 * 2:2], mixed[1:count // 2 * 2:2]
    slack = jnp.minimum(sizes[donor] - 1, bound - sizes[taker]) // 2
    slack = jnp.where((donor == order[0]) | (taker == order[0]) | (sizes[taker] == 0), 0, jnp.maximum(slack, 0))
    passed = jax.random.randint(jax.random.fold_in(own, 4), (count // 2,), 0, 1 << 20) % (slack + 1)
    sizes = sizes.at[donor].add(-passed).at[taker].add(passed)
    items = jnp.searchsorted(jnp.cumsum(sizes), jnp.arange(rows * top), side="right").astype(jnp.int32)
    listing = items.reshape(top, rows).T
    listing = listing[jax.random.permutation(jax.random.fold_in(own, 1), rows)]
    rotation = jax.random.randint(jax.random.fold_in(own, 2), (rows, 1), 0, top)
    return jnp.take_along_axis(listing, (jnp.arange(top)[None, :] + rotation) % top, axis=1)


def portions_of(number_of, total, reach, lean, full):
    portions = [(1 << 20) // math.isqrt(rank ** lean) + 1 for rank in range(1, number_of + 1)]
    largest = reach if full else min(reach, max(-(-total // number_of), total * portions[0] // sum(portions)))
    least = 1 if total - largest >= number_of - 1 else 0
    holding, surplus = [largest] + [least] * (number_of - 1), total - largest - least * (number_of - 1)
    while surplus > 0:
        candidates = [i for i in range(1, number_of) if holding[i] < largest] or [i for i in range(1, number_of) if holding[i] < reach]
        pool, left = sum([portions[i] for i in candidates]), surplus
        for i in candidates:
            addition = min(reach - holding[i], max(1, left * portions[i] // pool), surplus)
            holding[i] = holding[i] + addition
            surplus = surplus - addition
    return np.array(holding)


def scatter_about(own_key, extent, deviation, most, cuts=(), kind=jnp.bfloat16):
    array = jax.random.normal(own_key, extent, jnp.float32) * deviation
    if len(cuts) > 0:
        array = steps_of(own_key, extent, cuts, -0.22, 0.18) * array
    return jnp.clip(array, min=-most, max=most).astype(kind)


def setup_inputs(seed: int = 0) -> dict:
    splits = jax.random.split(jax.random.key(seed), 9)
    tokens = scatter_about(splits[0], (TOKENS, D), 1.0, 6.0, ((0, 16), (1, 2)))
    expert_ids_keys = jax.random.split(jax.random.fold_in(splits[1], 1), TOKENS // TOK_DEV)
    expert_ids_turns = jax.random.permutation(jax.random.fold_in(splits[1], 3), TOKENS // TOK_DEV)
    expert_ids = jax.vmap(lambda own, number: deal_out(jax.random.fold_in(splits[1], 2), own, number, TOK_DEV, EXPERTS, K, CAP + SPILL, 2))(expert_ids_keys, expert_ids_turns).reshape((TOKENS, K))
    gates = jnp.clip(0.1 + 0.5 * jax.random.uniform(splits[2], (TOKENS, K), jnp.float32) ** steps_of(splits[2], (TOKENS, K), ((0, 16),), -0.2, 0.2), 0.1, 0.6)
    cotangent = scatter_about(splits[3], (TOKENS, D), 0.1, 0.59765625, ((0, 16), (1, 2)))
    partner = draw_partner(jax.random.fold_in(splits[8], 71), 0)
    w_gate = scatter_about(splits[5], (EXPERTS, D, H), D ** -0.5, 0.09375, ((0, 16), (1, 2)))
    w_up = scatter_about(splits[6], (EXPERTS, D, H), D ** -0.5, 0.09375, ((0, 16), (1, 2)))
    w_down = scatter_about(splits[7], (EXPERTS, H, D), H ** -0.5, 0.1875, ((0, 16), (2, 2)))
    return dict(tokens=tokens, expert_ids=expert_ids, gates=gates, cotangent=cotangent, partner=partner, w_gate=w_gate, w_up=w_up, w_down=w_down)


def slot_ranks(expert_ids):
    blocks = expert_ids.reshape(N_EXPERT, TOK_DEV * K)
    labels = jnp.arange(EXPERTS, dtype=jnp.int32)
    onehot = (blocks[:, :, None] == labels[None, None, :]).astype(jnp.int32)
    counted = jnp.cumsum(onehot, axis=1) - 1
    return lax.optimization_barrier(jnp.sum(counted * onehot, axis=2)).reshape(TOKENS, K)

def piece_sums(left, weight):
    pieces = left.astype(jnp.float32).reshape(left.shape[0], N_DP, D // N_DP)
    wpieces = weight.astype(jnp.float32).reshape(N_DP, D // N_DP, H)
    terms = jnp.einsum('rsd,sdh->rsh', pieces, wpieces).astype(jnp.bfloat16)
    terms = lax.optimization_barrier(terms)
    return lax.optimization_barrier(jnp.sum(terms.astype(jnp.float32), axis=1))

def piece_sums_down(left, weight):
    pieces = left.astype(jnp.float32).reshape(left.shape[0], N_DP, D // N_DP)
    wpieces = weight.astype(jnp.float32).reshape(H, N_DP, D // N_DP)
    terms = jnp.einsum('rsd,hsd->rsh', pieces, wpieces).astype(jnp.bfloat16)
    terms = lax.optimization_barrier(terms)
    return lax.optimization_barrier(jnp.sum(terms.astype(jnp.float32), axis=1))

def split_grad(left, right):
    home_count = N_EXPERT * CAP
    home_sum = jnp.dot(left[:home_count].T, right[:home_count], preferred_element_type=jnp.float32)
    copy_sum = jnp.dot(left[home_count:].T, right[home_count:], preferred_element_type=jnp.float32).astype(jnp.bfloat16)
    copy_sum = lax.optimization_barrier(copy_sum)
    return (home_sum + copy_sum.astype(jnp.float32)).astype(jnp.bfloat16)

def reference(tokens, expert_ids, gates, cotangent, partner, w_gate, w_up, w_down):
    rank = slot_ranks(expert_ids)
    labels = jnp.arange(EXPERTS, dtype=jnp.int32)
    hosted = lax.optimization_barrier(jnp.sum((partner[:, None] == labels[None, :]).astype(jnp.int32), axis=0))
    pair_hosted = hosted[expert_ids]
    block = (jnp.arange(TOKENS, dtype=jnp.int32) // TOK_DEV)[:, None]
    home_count = N_EXPERT * CAP
    all_rows = N_EXPERT * (CAP + SPILL)
    dump = EXPERTS * all_rows
    home_place = expert_ids * all_rows + block * CAP + rank
    spill_place = expert_ids * all_rows + home_count + block * SPILL + rank - CAP
    place = jnp.where(rank < CAP, home_place, jnp.where(pair_hosted > 0, spill_place, dump))
    sentinel = TOKENS * K
    table = jnp.full((dump + 1,), sentinel, jnp.int32)
    table = table.at[place.reshape(-1)].set(jnp.arange(TOKENS * K, dtype=jnp.int32))
    table = table[:dump].reshape(EXPERTS, all_rows)
    tok_pad = jnp.concatenate([tokens, jnp.zeros((1, D), jnp.bfloat16)], axis=0)
    cot_pad = jnp.concatenate([cotangent, jnp.zeros((1, D), jnp.bfloat16)], axis=0)
    gate_pad = jnp.concatenate([gates.reshape(-1), jnp.zeros((1,), jnp.float32)], axis=0)

    def expert_step(carry, inputs):
        mixed, grad_tokens, grad_gates = carry
        slots, wg, wu, wd = inputs
        owner = slots // K
        xs = tok_pad[owner]
        weight_of = gate_pad[slots]
        cot_rows = cot_pad[owner].astype(jnp.float32)
        dout = (weight_of[:, None] * cot_rows).astype(jnp.bfloat16)
        gate_pre = piece_sums(xs, wg)
        up_pre = piece_sums(xs, wu)
        dhid = piece_sums_down(dout, wd)
        sig = jax.nn.sigmoid(gate_pre)
        act = gate_pre * sig
        hid = (act * up_pre).astype(jnp.bfloat16)
        dup = (dhid * act).astype(jnp.bfloat16)
        dgate = (dhid * up_pre * sig * (1.0 + gate_pre * (1.0 - sig))).astype(jnp.bfloat16)
        out = jnp.dot(hid, wd, preferred_element_type=jnp.float32).astype(jnp.bfloat16)
        dxs = (jnp.dot(dgate, wg.T, preferred_element_type=jnp.float32) + jnp.dot(dup, wu.T, preferred_element_type=jnp.float32)).astype(jnp.bfloat16)
        grad_down = split_grad(hid, dout)
        grad_gate = split_grad(xs, dgate)
        grad_up = split_grad(xs, dup)
        outf = out.astype(jnp.float32)
        mixed = mixed.at[owner].add(weight_of[:, None] * outf)
        grad_tokens = grad_tokens.at[owner].add(dxs.astype(jnp.float32))
        grad_gates = grad_gates.at[slots].set(lax.optimization_barrier(jnp.sum(cot_rows * outf, axis=1)))
        return ((mixed, grad_tokens, grad_gates), (grad_gate, grad_up, grad_down))
    start = (jnp.zeros((TOKENS + 1, D), jnp.float32), jnp.zeros((TOKENS + 1, D), jnp.float32), jnp.zeros((TOKENS * K + 1,), jnp.float32))
    final, grads = lax.scan(expert_step, start, (table, w_gate, w_up, w_down))
    mixed, grad_tokens, grad_gates = final
    return (mixed[:TOKENS].astype(jnp.bfloat16), grad_tokens[:TOKENS].astype(jnp.bfloat16), grad_gates[:TOKENS * K].reshape(TOKENS, K), grads[0], grads[1], grads[2])
```

```python
import functools

import jax
import jax.numpy as jnp
from jax import lax
from jax.experimental import pallas as pl
from jax.experimental.pallas import tpu as pltpu
from jax.sharding import PartitionSpec as P

F32, BF16 = jnp.float32, jnp.bfloat16
MESH = pl.DeviceIdType.MESH
TILE = 256


def dot(left, right, dims):
    return lax.dot_general(left, right, (dims, ((), ())), preferred_element_type=jnp.float32)


def rows_of(onehot, values):
    rows = lax.dot_general(
        onehot, values, (((2,), (1,)), ((0,), (0,))), preferred_element_type=jnp.float32
    )
    return rows.astype(jnp.bfloat16).reshape(-1, values.shape[2])


def ring_kernel(
    n_exp, rows, top, cap, slots, width, hidden,
    small, partner, tokens, cot, w_gate, w_up, w_down,
    mixed, grad_tokens, grad_gates, g_gate, g_up, g_down, held, other, sib_in, ring_in,
    wg, wu, wd, blk, xc, pre, far, sib_out, tmp, stage,
    sm_held, sm_other, sm_acc, sm_sib_out, sm_sib_in, sm_ring_in,
    sgate, sacc, back,
    load_sem, ag_s, ag_r, sg_s, sg_r, mag_s, mag_r, msg_s, msg_r,
    x_s, x_r, sp_s, sp_r, msp_s, msp_r, rp_s, rp_r, mrp_s, mrp_r,
):
    chips = n_exp // 2
    half = chips // 2
    pair = 2 * slots
    per = hidden // TILE
    cols = width // TILE

    dp = lax.axis_index("dp")
    me = lax.axis_index("expert")
    core = me % 2
    chip = me // 2
    y, z = chip % 2, chip // 2
    spot = z + y * (chips - 1 - 2 * z)

    def at_spot(q):
        q = q % chips
        hi = q // half
        return 2 * (2 * (q + hi * (chips - 1 - 2 * q)) + hi) + core

    ahead = (dp, at_spot(spot + 1))
    behind = (dp, at_spot(spot + chips - 1))
    sibling = (dp, me + 1 - 2 * core)
    across = (1 - dp, me)
    turn = (dp, ahead[1] + core * (behind[1] - ahead[1]))

    def remote(src, dst, send, recv, to):
        return pltpu.make_async_remote_copy(
            src_ref=src, dst_ref=dst, send_sem=send, recv_sem=recv,
            device_id=to, device_id_type=MESH,
        )

    def ring_copies(src, dst, to):
        return (
            remote(held.at[src], held.at[dst], ag_s.at[dst], ag_r.at[dst], to),
            remote(sm_held.at[src], sm_held.at[dst], mag_s.at[dst], mag_r.at[dst], to),
        )

    def side_copies(u):
        return (
            remote(held.at[u], other.at[u], sg_s.at[u], sg_r.at[u], sibling),
            remote(sm_held.at[u], sm_other.at[u], msg_s.at[u], msg_r.at[u], sibling),
        )

    def x_copy(u):
        return remote(pre.at[u], far.at[u], x_s.at[u], x_r.at[u], across)

    def part_copies(u):
        return (
            remote(sib_out.at[u % 2], sib_in.at[u], sp_s.at[u], sp_r.at[u], sibling),
            remote(sm_sib_out.at[u], sm_sib_in.at[u], msp_s.at[u], msp_r.at[u], sibling),
        )

    def home_copies(u, dst, to):
        return (
            remote(far.at[u, pl.ds(0, 4 * rows)], ring_in.at[dst], rp_s.at[dst], rp_r.at[dst], to),
            remote(sm_acc.at[u], sm_ring_in.at[dst], mrp_s.at[dst], mrp_r.at[dst], to),
        )

    def start(copies):
        for copy in copies:
            copy.start()

    def wait_recv(copies):
        for copy in copies:
            copy.wait_recv()

    def wait_send(copies):
        for copy in copies:
            copy.wait_send()

    own = (
        pltpu.make_async_copy(tokens, held.at[0, :, pl.ds(0, width)], load_sem.at[0]),
        pltpu.make_async_copy(cot, held.at[0, :, pl.ds(width, width)], load_sem.at[1]),
    )
    weights = (
        pltpu.make_async_copy(w_gate, wg, load_sem.at[2]),
        pltpu.make_async_copy(w_up, wu, load_sem.at[3]),
        pltpu.make_async_copy(w_down, wd, load_sem.at[4]),
    )
    start(own)
    sm_held[0] = small[...]

    barrier = pltpu.get_barrier_semaphore()
    for to in (ahead, behind, sibling, across):
        pl.semaphore_signal(barrier, inc=1, device_id=to, device_id_type=MESH)
    pl.semaphore_wait(barrier, 4)

    for copy in own:
        copy.wait()
    start(side_copies(0))
    start(ring_copies(0, 1, behind))
    start(ring_copies(0, chips - 1, ahead))
    start(weights)

    me_f = me.astype(F32)
    hosted = jnp.max(jnp.where(partner[...] == me, 1.0, 0.0), axis=1, keepdims=True)
    limit = slots - (1.0 - hosted) * (slots - cap)

    def routes(info):
        ids, gates = info[:top], info[top:]
        hit = ids == me_f
        present = jnp.max(jnp.where(hit, 1.0, 0.0), axis=0, keepdims=True)
        gate = jnp.sum(jnp.where(hit, gates, 0.0), axis=0, keepdims=True)
        earlier = (
            lax.broadcasted_iota(jnp.int32, (rows, rows), 0)
            < lax.broadcasted_iota(jnp.int32, (rows, rows), 1)
        ).astype(F32).astype(BF16)
        spread = jnp.broadcast_to(present, (16, rows)).astype(BF16)
        rank = dot(spread, earlier, ((1,), (0,)))[:1]
        taken = jnp.where(rank < limit, present, 0.0)
        place = jnp.where(taken > 0.0, rank, -1.0)
        index = lax.broadcasted_iota(jnp.int32, (rows, rows), 0).astype(F32)
        match = jnp.where(index == place, 1.0, 0.0)
        return hit, gate, match

    def info_of(u, b):
        return (sm_held, sm_other)[b][u]

    def forward(step):
        arrived = [step] if step == half else [step, chips - step]
        for v in arrived:
            wait_recv(ring_copies(v, v, behind))
        if step < half - 1:
            start(ring_copies(step, step + 1, behind))
            start(ring_copies(chips - step, chips - step - 1, ahead))
        elif step == half - 1:
            start(ring_copies(half + 1 - 2 * core, half, turn))
        for v in arrived:
            start(side_copies(v))

    def project(u):
        wait_recv(side_copies(u))
        loads = [
            pltpu.make_async_copy(source.at[u], blk.at[b], load_sem.at[b])
            for b, source in enumerate((held, other))
        ]
        start(loads)
        picks = []
        for b in range(2):
            _, _, match = routes(info_of(u, b))
            picks.append(match.astype(BF16)[:slots])
        for copy in loads:
            copy.wait()
        first = pl.multiple_of(u * pair, pair)

        def gather(n, _):
            column = pl.ds(pl.multiple_of(n * 2 * TILE, 2 * TILE), 2 * TILE)
            for b in range(2):
                got = dot(picks[b], blk[b, :, column], ((1,), (0,)))
                xc[pl.ds(pl.multiple_of(first + b * slots, slots), slots), column] = got.astype(BF16)
            return 0

        lax.fori_loop(0, cols, gather, 0)
        band = pl.ds(first, pair)

        def product(n, _):
            column = pl.ds(pl.multiple_of(n * TILE, TILE), TILE)
            xs = xc[band, pl.ds(0, width)]
            pre[u, pl.ds(0, pair), column] = dot(xs, wg[:, column], ((1,), (0,))).astype(BF16)
            pre[u, pl.ds(pair, pair), column] = dot(xs, wu[:, column], ((1,), (0,))).astype(BF16)
            cs = xc[band, pl.ds(width, width)]
            pre[u, pl.ds(2 * pair, pair), column] = dot(cs, wd[column, :], ((1,), (1,))).astype(BF16)
            return 0

        lax.fori_loop(0, per, product, 0)
        x_copy(u).start()

    def respond(u):
        hits = []
        matches = []
        for b in range(2):
            hit, gate, match = routes(info_of(u, b))
            weight = jnp.sum(match * gate, axis=1, keepdims=True)
            sgate[pl.ds(b * slots, slots)] = jnp.broadcast_to(weight[:slots], (slots, 128))
            back[b] = match.T.astype(BF16)
            hits.append(hit)
            matches.append(match[:slots])
        sacc[...] = jnp.zeros_like(sacc)
        x_copy(u).wait()

        def activate(n, _):
            column = pl.ds(pl.multiple_of(n * 128, 128), 128)

            def total(k):
                part = pl.ds(k * pair, pair)
                return pre[u, part, column].astype(F32) + far[u, part, column].astype(F32)

            gate_pre, up_pre, raw = total(0), total(1), total(2)
            sig = 1.0 / (1.0 + jnp.exp(-gate_pre))
            act = gate_pre * sig
            hid = act * up_pre
            scale = sgate[...]
            dhid = scale * raw
            sacc[...] += hid * raw
            pre[u, pl.ds(0, pair), column] = (scale * hid).astype(BF16)
            pre[u, pl.ds(pair, pair), column] = (dhid * act).astype(BF16)
            slope = sig * (1.0 + gate_pre * (1.0 - sig))
            pre[u, pl.ds(2 * pair, pair), column] = (dhid * up_pre * slope).astype(BF16)
            return 0

        lax.fori_loop(0, hidden // 128, activate, 0)

        for b in range(2):
            term = jnp.sum(sacc[pl.ds(b * slots, slots)], axis=1, keepdims=True)
            spread = jnp.sum(matches[b] * term, axis=0, keepdims=True)
            (sm_acc, sm_sib_out)[b][u] = jnp.where(hits[b], spread, 0.0)

        @pl.when(u >= 2)
        def _():
            part_copies(u - 2)[0].wait_send()

        def emit(n, _):
            column = pl.ds(pl.multiple_of(n * TILE, TILE), TILE)
            out = dot(pre[u, pl.ds(0, pair)], wd[:, column], ((1,), (0,))).astype(BF16)
            dx = (
                dot(pre[u, pl.ds(2 * pair, pair)], wg[column, :], ((1,), (1,)))
                + dot(pre[u, pl.ds(pair, pair)], wu[column, :], ((1,), (1,)))
            ).astype(BF16)
            lane = pl.ds(pl.multiple_of(n % per * TILE, TILE), TILE)
            for k, value in enumerate((out, dx)):
                low = pl.multiple_of((2 * k + n // per) * rows, rows)
                for b in range(2):
                    home = dot(
                        back[b][:, :slots], value[b * slots:(b + 1) * slots], ((1,), (0,))
                    ).astype(BF16)
                    if b == 0:
                        far[u, pl.ds(low, rows), lane] = home
                    else:
                        sib_out[u % 2, pl.ds(low, rows), lane] = home
            return 0

        lax.fori_loop(0, cols, emit, 0)
        start(part_copies(u))

    chunk = 64

    def combine(u, incoming):
        loads = [pltpu.make_async_copy(sib_in.at[u], tmp.at[0], load_sem.at[0])]
        wait_recv(part_copies(u))
        loads[0].start()
        totals = sm_acc[u] + sm_sib_in[u]
        for k, slot in enumerate(incoming):
            wait_recv(home_copies(u, slot, behind))
            loads.append(pltpu.make_async_copy(ring_in.at[slot], tmp.at[k + 1], load_sem.at[k + 1]))
            loads[-1].start()
            totals = totals + sm_ring_in[slot]
        for copy in loads:
            copy.wait()
        sm_acc[u] = totals

        def add(n, _):
            part = pl.ds(pl.multiple_of(n * chunk, chunk), chunk)
            total = far[u, part].astype(F32)
            for k in range(len(loads)):
                total = total + tmp[k, part].astype(F32)
            far[u, part] = total.astype(BF16)
            return 0

        lax.fori_loop(0, 4 * rows // chunk, add, 0)

    def send_home(u):
        if u == half:
            combine(u, [])
            start(home_copies(u, half - 1 + 2 * core, turn))
        elif u < half:
            if u == half - 1:
                pl.when(core == 0)(lambda: combine(u, [u]))
                pl.when(core == 1)(lambda: combine(u, []))
            else:
                combine(u, [u])
            start(home_copies(u, u - 1, ahead))
        else:
            if u == half + 1:
                pl.when(core == 1)(lambda: combine(u, [u]))
                pl.when(core == 0)(lambda: combine(u, []))
            else:
                combine(u, [u])
            start(home_copies(u, u + 1, behind))

    def turn_of(i, _):
        for step in range(1, half + 1):
            pl.when(i == step)(functools.partial(forward, step))

        @pl.when(i == 0)
        def _():
            for copy in weights:
                copy.wait()

        pl.when(i < chips)(lambda: project(i))
        for k in range(1, half):
            pl.when(i == half + 1 + k)(functools.partial(send_home, half - k))
        pl.when(i > 0)(lambda: respond(i - 1))
        for k in range(half):
            pl.when(i == half + 1 + k)(functools.partial(send_home, half + k))
        return 0

    lax.fori_loop(0, chips + 1, turn_of, 0)

    def gradient(target, left_of, right_of, put):
        def step(n, _):
            slot = n % 2

            @pl.when(n >= 2)
            def _():
                pltpu.make_async_copy(stage.at[slot], put(target, n - 2), load_sem.at[slot]).wait()

            stage[slot] = dot(left_of(n), right_of(n), ((0,), (0,))).astype(BF16)
            pltpu.make_async_copy(stage.at[slot], put(target, n), load_sem.at[slot]).start()
            return 0

        lax.fori_loop(0, cols, step, 0)
        for n in (cols - 2, cols - 1):
            pltpu.make_async_copy(stage.at[n % 2], put(target, n), load_sem.at[n % 2]).wait()

    def whole(k, column):
        return pre[:, pl.ds(k * pair, pair), column].reshape(chips * pair, -1)

    def tile_of(n, size=TILE):
        return pl.ds(pl.multiple_of(n * size, size), size)

    for target, k in ((g_gate, 2), (g_up, 1)):
        gradient(
            target,
            lambda n: xc[:, tile_of(n)],
            lambda n, k=k: whole(k, pl.ds(0, hidden)),
            lambda ref, n: ref.at[tile_of(n)],
        )
    parts = width // hidden
    gradient(
        g_down,
        lambda n: whole(0, tile_of(n // parts)),
        lambda n: xc[:, pl.ds(pl.multiple_of(width + n % parts * hidden, hidden), hidden)],
        lambda ref, n: ref.at[tile_of(n // parts), tile_of(n % parts, hidden)],
    )

    combine(0, [0, chips])
    grad_gates[...] = sm_acc[0]
    for k, target in enumerate((mixed, grad_tokens)):
        for part in range(2):
            target[:, part * hidden:(part + 1) * hidden] = far[0, (2 * k + part) * rows:(2 * k + part + 1) * rows]

    for v in range(1, chips):
        wait_send(ring_copies(v, v, behind))
    for u in range(chips):
        wait_send(side_copies(u))
        copies = part_copies(u)
        if u >= chips - 2:
            copies[0].wait_send()
        copies[1].wait_send()
    for slot in range(chips + 1):
        if slot not in (half - 1, half, half + 1):
            wait_send(home_copies(0, slot, behind))
    wait_send(home_copies(0, half - 1 + 2 * core, turn))


def ring_local(tokens, expert_ids, gates, cotangent, partner, w_gate, w_up, w_down):
    n_exp = lax.axis_size("expert")
    rows, width = tokens.shape
    hidden = w_gate.shape[2]
    top = expert_ids.shape[1]
    cap = rows * top // n_exp
    slots = cap + cap // 2
    chips = n_exp // 2
    pair = 2 * slots
    fits = width == 2 * hidden and hidden % TILE == 0 and slots % 16 == 0
    if not fits or rows != 128 or slots > rows or 4 * rows > 3 * pair or top % 8:
        return local(tokens, expert_ids, gates, cotangent, partner, w_gate, w_up, w_down)
    small = jnp.concatenate([expert_ids.T.astype(F32), gates.T], axis=0)

    anywhere = pl.BlockSpec(memory_space=pl.ANY)
    inside = pl.BlockSpec(memory_space=pltpu.VMEM)
    shape = jax.ShapeDtypeStruct
    dma = pltpu.SemaphoreType.DMA
    vmem = pltpu.VMEM
    outs = pl.pallas_call(
        functools.partial(ring_kernel, n_exp, rows, top, cap, slots, width, hidden),
        out_shape=(
            shape((rows, width), BF16),
            shape((rows, width), BF16),
            shape((top, rows), F32),
            shape((width, hidden), BF16),
            shape((width, hidden), BF16),
            shape((hidden, width), BF16),
            shape((chips, rows, 2 * width), BF16),
            shape((chips, rows, 2 * width), BF16),
            shape((chips, 4 * rows, hidden), BF16),
            shape((chips + 1, 4 * rows, hidden), BF16),
        ),
        in_specs=[inside] * 2 + [anywhere] * 5,
        out_specs=(inside,) * 3 + (anywhere,) * 7,
        scratch_shapes=[
            vmem((width, hidden), BF16),
            vmem((width, hidden), BF16),
            vmem((hidden, width), BF16),
            vmem((2, rows, 2 * width), BF16),
            vmem((chips * pair, 2 * width), BF16),
            vmem((chips, 3 * pair, hidden), BF16),
            vmem((chips, 3 * pair, hidden), BF16),
            vmem((2, 4 * rows, hidden), BF16),
            vmem((3, 4 * rows, hidden), BF16),
            vmem((2, TILE, hidden), BF16),
            vmem((chips, 2 * top, rows), F32),
            vmem((chips, 2 * top, rows), F32),
            vmem((chips, top, rows), F32),
            vmem((chips, top, rows), F32),
            vmem((chips, top, rows), F32),
            vmem((chips + 1, top, rows), F32),
            vmem((pair, 128), F32),
            vmem((pair, 128), F32),
            vmem((2, rows, rows), BF16),
            dma((5,)),
        ] + [dma((chips,))] * 14 + [dma((chips + 1,))] * 4,
        compiler_params=pltpu.CompilerParams(
            collective_id=0, has_side_effects=True, vmem_limit_bytes=60 * 1024 * 1024
        ),
        cost_estimate=pl.CostEstimate(
            flops=18 * chips * pair * width * hidden,
            bytes_accessed=12 * width * hidden,
            transcendentals=chips * pair * hidden,
        ),
    )(small, partner.reshape(1, -1), tokens, cotangent, w_gate[0], w_up[0], w_down[0])
    mixed, grad_tokens, grad_gates, g_gate, g_up, g_down = outs[:6]
    return mixed, grad_tokens, grad_gates.T, g_gate[None], g_up[None], g_down[None]


def local(tokens, expert_ids, gates, cotangent, partner, w_gate, w_up, w_down):
    n_exp = lax.axis_size("expert")
    n_dp = lax.axis_size("dp")
    me = lax.axis_index("expert")
    rows, width = tokens.shape
    top = expert_ids.shape[1]
    cap = rows * top // n_exp
    slots = cap + cap // 2
    own_gate, own_up, own_down = w_gate[0], w_up[0], w_down[0]

    small = jnp.concatenate([expert_ids.T.astype(jnp.float32), gates.T], axis=0)
    small = lax.all_gather(small, "expert", axis=0, tiled=False)
    all_x = lax.all_gather(tokens, "expert", axis=0, tiled=False)
    later, all_x = lax.optimization_barrier((cotangent, all_x))
    all_c = lax.all_gather(later, "expert", axis=0, tiled=False)

    hit = small[:, :top] == me.astype(jnp.float32)
    present = jnp.any(hit, axis=1)
    token_gate = jnp.sum(jnp.where(hit, small[:, top:], 0.0), axis=1)
    order = jnp.arange(rows)
    earlier = (order[:, None] < order[None, :]).astype(jnp.bfloat16)
    rank = dot(present.astype(jnp.bfloat16), earlier, ((1,), (0,))).astype(jnp.int32)
    limit = jnp.where(jnp.any(partner == me), slots, cap)
    taken = jnp.logical_and(present, rank < limit)
    place = jnp.where(taken, rank, -1)
    match = place[:, None, :] == jnp.arange(slots)[None, :, None]
    onehot = match.astype(jnp.bfloat16)
    slot_gate = jnp.sum(jnp.where(match, token_gate[:, None, :], 0.0), axis=2).reshape(-1, 1)
    back = (jnp.arange(slots)[None, None, :] == place[:, :, None]).astype(jnp.bfloat16)

    xs = rows_of(onehot, all_x)
    pre_g = dot(xs, own_gate, ((1,), (0,))).astype(jnp.bfloat16)
    pre_u = dot(xs, own_up, ((1,), (0,))).astype(jnp.bfloat16)
    cs = rows_of(onehot, all_c)
    pre_d = dot(cs, own_down, ((1,), (1,))).astype(jnp.bfloat16)

    if n_dp == 2:
        swap = [(0, 1), (1, 0)]

        def exchange(part):
            return (part, lax.ppermute(part, "dp", swap))

        def summed(both):
            return both[0].astype(jnp.float32) + both[1].astype(jnp.float32)

        def full(part):
            return part
    else:

        def exchange(part):
            return (lax.psum_scatter(part, "dp", scatter_dimension=1, tiled=True),)

        def summed(both):
            return both[0].astype(jnp.float32)

        def full(part):
            return lax.all_gather(part, "dp", axis=1, tiled=True)

    sum_g = exchange(pre_g)
    sum_u = exchange(pre_u)
    sum_d = exchange(pre_d)
    sum_g, sum_u, _ = lax.optimization_barrier((sum_g, sum_u, pre_d))
    gate_pre = summed(sum_g)
    up_pre = summed(sum_u)
    sig = jax.nn.sigmoid(gate_pre)
    act = gate_pre * sig
    hid = act * up_pre
    scaled_hid = full((slot_gate * hid).astype(jnp.bfloat16))

    def to_tokens(slot_rows):
        return rows_of(back, slot_rows.reshape(n_exp, slots, width))

    def send_home(parts):
        return lax.psum_scatter(parts, "expert", scatter_dimension=0, tiled=True)

    out = dot(scaled_hid, own_down, ((1,), (0,))).astype(jnp.bfloat16)
    out_parts = to_tokens(out)
    mixed = send_home(out_parts)

    sum_d, sum_g, sum_u, _ = lax.optimization_barrier((sum_d, sum_g, sum_u, out_parts))
    gate_pre = summed(sum_g)
    up_pre = summed(sum_u)
    sig = jax.nn.sigmoid(gate_pre)
    act = gate_pre * sig
    hid = act * up_pre
    raw = summed(sum_d)
    dhid = slot_gate * raw
    dup = full((dhid * act).astype(jnp.bfloat16))
    dgate = full((dhid * up_pre * sig * (1.0 + gate_pre * (1.0 - sig))).astype(jnp.bfloat16))
    slot_terms = jnp.sum(hid * raw, axis=1).reshape(n_exp, 1, slots)
    dx = (dot(dgate, own_gate, ((1,), (1,))) + dot(dup, own_up, ((1,), (1,)))).astype(jnp.bfloat16)
    grad_tokens = send_home(to_tokens(dx))

    mine = place[:, :, None] == jnp.arange(slots)[None, None, :]
    terms = jnp.sum(jnp.where(mine, slot_terms, 0.0), axis=2)
    terms = lax.all_to_all(terms, "expert", split_axis=0, concat_axis=0, tiled=True)
    labels = jnp.arange(n_exp, dtype=jnp.int32)
    chosen = expert_ids.T[None, :, :] == labels[:, None, None]
    grad_gates = jnp.sum(jnp.where(chosen, terms[:, None, :], 0.0), axis=0).T
    if n_dp != 2:
        grad_gates = lax.psum(grad_gates, "dp")

    grad_down = dot(scaled_hid, cs, ((0,), (0,))).astype(jnp.bfloat16)
    grad_up = dot(xs, dup, ((0,), (0,))).astype(jnp.bfloat16)
    grad_gate = dot(xs, dgate, ((0,), (0,))).astype(jnp.bfloat16)
    return (mixed, grad_tokens, grad_gates, grad_gate[None], grad_up[None], grad_down[None])


def solution(mesh):
    placed = (
        P("expert", "dp"),
        P("expert", None),
        P("expert", None),
        P("expert", "dp"),
        P(),
        P("expert", "dp", None),
        P("expert", "dp", None),
        P("expert", None, "dp"),
    )
    paired = mesh.shape["dp"] == 2 and mesh.shape["expert"] % 4 == 0
    return jax.shard_map(
        ring_local if paired else local,
        mesh=mesh,
        in_specs=placed,
        out_specs=(
            P("expert", "dp"),
            P("expert", "dp"),
            P("expert", None),
            P("expert", "dp", None),
            P("expert", "dp", None),
            P("expert", None, "dp"),
        ),
        check_vma=False,
    )
```

```python
import functools

import jax
import jax.numpy as jnp
from jax import lax
from jax.experimental import pallas as pl
from jax.experimental.pallas import tpu as pltpu
from jax.sharding import PartitionSpec as P

F32, BF16 = jnp.float32, jnp.bfloat16
MESH = pl.DeviceIdType.MESH
TILE = 256


def dot(left, right, dims):
    return lax.dot_general(left, right, (dims, ((), ())), preferred_element_type=jnp.float32)


def rows_of(onehot, values):
    rows = lax.dot_general(
        onehot, values, (((2,), (1,)), ((0,), (0,))), preferred_element_type=jnp.float32
    )
    return rows.astype(jnp.bfloat16).reshape(-1, values.shape[2])


def ring_kernel(
    n_exp, rows, top, cap, slots, width, hidden,
    small, partner, tokens, cot, w_gate, w_up, w_down,
    mixed, grad_tokens, grad_gates, g_gate, g_up, g_down, held, other, sib_in, ring_in,
    wg, wu, wd, blk, xc, pre, far, sib_out, tmp, stage,
    sm_held, sm_other, sm_acc, sm_sib_out, sm_sib_in, sm_ring_in,
    sgate, sacc, back, picks,
    load_sem, ag_s, ag_r, sg_s, sg_r, mag_s, mag_r, msg_s, msg_r,
    x_s, x_r, sp_s, sp_r, msp_s, msp_r, rp_s, rp_r, mrp_s, mrp_r,
):
    chips = n_exp // 2
    half = chips // 2
    pair = 2 * slots
    per = hidden // TILE
    cols = width // TILE

    dp = lax.axis_index("dp")
    me = lax.axis_index("expert")
    core = me % 2
    chip = me // 2
    y, z = chip % 2, chip // 2
    spot = z + y * (chips - 1 - 2 * z)

    def at_spot(q):
        q = q % chips
        hi = q // half
        return 2 * (2 * (q + hi * (chips - 1 - 2 * q)) + hi) + core

    ahead = (dp, at_spot(spot + 1))
    behind = (dp, at_spot(spot + chips - 1))
    sibling = (dp, me + 1 - 2 * core)
    across = (1 - dp, me)
    turn = (dp, ahead[1] + core * (behind[1] - ahead[1]))

    def remote(src, dst, send, recv, to):
        return pltpu.make_async_remote_copy(
            src_ref=src, dst_ref=dst, send_sem=send, recv_sem=recv,
            device_id=to, device_id_type=MESH,
        )

    def ring_copies(src, dst, to, block=None):
        block = held.at[src] if block is None else block
        return (
            remote(block, held.at[dst], ag_s.at[dst], ag_r.at[dst], to),
            remote(sm_held.at[src], sm_held.at[dst], mag_s.at[dst], mag_r.at[dst], to),
        )

    def side_copies(u, block=None):
        block = held.at[u] if block is None else block
        return (
            remote(block, other.at[u], sg_s.at[u], sg_r.at[u], sibling),
            remote(sm_held.at[u], sm_other.at[u], msg_s.at[u], msg_r.at[u], sibling),
        )

    def x_copy(u, k):
        part = pl.ds(k * pair, pair)
        return remote(pre.at[u, part], far.at[u, part], x_s.at[k, u], x_r.at[k, u], across)

    def part_copies(u):
        return (
            remote(sib_out.at[u % 2], sib_in.at[u], sp_s.at[u], sp_r.at[u], sibling),
            remote(sm_sib_out.at[u], sm_sib_in.at[u], msp_s.at[u], msp_r.at[u], sibling),
        )

    def home_copies(u, dst, to):
        return (
            remote(far.at[u, pl.ds(0, 4 * rows)], ring_in.at[dst], rp_s.at[dst], rp_r.at[dst], to),
            remote(sm_acc.at[u], sm_ring_in.at[dst], mrp_s.at[dst], mrp_r.at[dst], to),
        )

    def start(copies):
        for copy in copies:
            copy.start()

    def wait_recv(copies):
        for copy in copies:
            copy.wait_recv()

    def wait_send(copies):
        for copy in copies:
            copy.wait_send()

    own = (
        pltpu.make_async_copy(tokens, blk.at[pl.ds(0, rows), pl.ds(0, width)], load_sem.at[0]),
        pltpu.make_async_copy(cot, blk.at[pl.ds(0, rows), pl.ds(width, width)], load_sem.at[1]),
    )
    weights = (
        pltpu.make_async_copy(w_gate, wg, load_sem.at[2]),
        pltpu.make_async_copy(w_up, wu, load_sem.at[3]),
        pltpu.make_async_copy(w_down, wd, load_sem.at[4]),
    )
    start(own)
    start(weights)
    sm_held[0] = small[...]

    barrier = pltpu.get_barrier_semaphore()
    for to in (ahead, behind, sibling, across):
        pl.semaphore_signal(barrier, inc=1, device_id=to, device_id_type=MESH)
    pl.semaphore_wait(barrier, 4)

    for copy in own:
        copy.wait()
    start(side_copies(0, blk.at[pl.ds(0, rows)]))
    start(ring_copies(0, 1, behind, blk.at[pl.ds(0, rows)]))
    start(ring_copies(0, chips - 1, ahead, blk.at[pl.ds(0, rows)]))

    me_f = me.astype(F32)
    hosted = jnp.max(jnp.where(partner[...] == me, 1.0, 0.0), axis=1, keepdims=True)
    limit = slots - (1.0 - hosted) * (slots - cap)

    def routes(info):
        ids, gates = info[:top], info[top:]
        hit = ids == me_f
        present = jnp.max(jnp.where(hit, 1.0, 0.0), axis=0, keepdims=True)
        gate = jnp.sum(jnp.where(hit, gates, 0.0), axis=0, keepdims=True)
        earlier = (
            lax.broadcasted_iota(jnp.int32, (rows, rows), 0)
            < lax.broadcasted_iota(jnp.int32, (rows, rows), 1)
        ).astype(F32).astype(BF16)
        spread = jnp.broadcast_to(present, (16, rows)).astype(BF16)
        rank = dot(spread, earlier, ((1,), (0,)))[:1]
        taken = jnp.where(rank < limit, present, 0.0)
        place = jnp.where(taken > 0.0, rank, -1.0)
        index = lax.broadcasted_iota(jnp.int32, (rows, rows), 0).astype(F32)
        match = jnp.where(index == place, 1.0, 0.0)
        return hit, gate, match

    def diagonal(matches):
        low = jnp.zeros((slots, rows), F32)
        left = jnp.concatenate([matches[0][:slots], low], axis=0)
        right = jnp.concatenate([low, matches[1][:slots]], axis=0)
        both = jnp.concatenate([left, right], axis=1)
        return jnp.concatenate([both, jnp.zeros((2 * (rows - slots), 2 * rows), F32)], axis=0)

    def info_of(u, b):
        return (sm_held, sm_other)[b][u]

    def forward(step):
        arrived = [step] if step == half else [step, chips - step]
        for v in arrived:
            wait_recv(ring_copies(v, v, behind))
        if step == 1:
            wait_send(side_copies(0) + ring_copies(0, 1, behind) + ring_copies(0, chips - 1, ahead))
        if step < half - 1:
            start(ring_copies(step, step + 1, behind))
            start(ring_copies(chips - step, chips - step - 1, ahead))
        elif step == half - 1:
            start(ring_copies(half + 1 - 2 * core, half, turn))
        for v in arrived:
            start(side_copies(v))

    def project(u):
        wait_recv(side_copies(u))
        loads = [
            pltpu.make_async_copy(source.at[u], blk.at[pl.ds(b * rows, rows)], load_sem.at[b])
            for b, source in enumerate((held, other))
        ]

        @pl.when(u > 0)
        def _():
            loads[0].start()

        loads[1].start()
        picks[...] = diagonal([routes(info_of(u, b))[2] for b in range(2)])[:pair].astype(BF16)
        pl.when(u > 0)(lambda: loads[0].wait())
        loads[1].wait()
        first = pl.multiple_of(u * pair, pair)

        def gather(n, _):
            column = pl.ds(pl.multiple_of(n * 2 * TILE, 2 * TILE), 2 * TILE)
            xc[pl.ds(first, pair), column] = dot(picks[...], blk[:, column], ((1,), (0,))).astype(BF16)
            return 0

        lax.fori_loop(0, cols, gather, 0, unroll=4)
        band = pl.ds(first, pair)

        for k in range(3):
            pl.when(u == 0)(lambda k=k: weights[k].wait())
            part = pl.ds(k * pair, pair)

            def product(n, _):
                column = pl.ds(pl.multiple_of(n * TILE, TILE), TILE)
                if k < 2:
                    got = dot(xc[band, pl.ds(0, width)], (wg, wu)[k][:, column], ((1,), (0,)))
                else:
                    got = dot(xc[band, pl.ds(width, width)], wd[column, :], ((1,), (1,)))
                pre[u, part, column] = got.astype(BF16)
                return 0

            lax.fori_loop(0, per, product, 0, unroll=4)
            x_copy(u, k).start()

    def respond(u):
        hits = []
        matches = []
        for b in range(2):
            hit, gate, match = routes(info_of(u, b))
            weight = jnp.sum(match * gate, axis=1, keepdims=True)
            sgate[pl.ds(b * slots, slots)] = jnp.broadcast_to(weight[:slots], (slots, 128))
            hits.append(hit)
            matches.append(match[:slots])
        back[...] = diagonal(matches).T.astype(BF16)
        sacc[...] = jnp.zeros_like(sacc)
        for k in range(3):
            x_copy(u, k).wait()

        def activate(n, _):
            column = pl.ds(pl.multiple_of(n * 128, 128), 128)

            def total(k):
                part = pl.ds(k * pair, pair)
                return pre[u, part, column].astype(F32) + far[u, part, column].astype(F32)

            gate_pre, up_pre, raw = total(0), total(1), total(2)
            sig = 1.0 / (1.0 + jnp.exp(-gate_pre))
            act = gate_pre * sig
            hid = act * up_pre
            scale = sgate[...]
            dhid = scale * raw
            sacc[...] += hid * raw
            pre[u, pl.ds(0, pair), column] = (scale * hid).astype(BF16)
            pre[u, pl.ds(pair, pair), column] = (dhid * act).astype(BF16)
            slope = sig * (1.0 + gate_pre * (1.0 - sig))
            pre[u, pl.ds(2 * pair, pair), column] = (dhid * up_pre * slope).astype(BF16)
            return 0

        lax.fori_loop(0, hidden // 128, activate, 0)

        for b in range(2):
            term = jnp.sum(sacc[pl.ds(b * slots, slots)], axis=1, keepdims=True)
            spread = jnp.sum(matches[b] * term, axis=0, keepdims=True)
            (sm_acc, sm_sib_out)[b][u] = jnp.where(hits[b], spread, 0.0)

        @pl.when(u >= 2)
        def _():
            part_copies(u - 2)[0].wait_send()

        def emit(n, _):
            column = pl.ds(pl.multiple_of(n * TILE, TILE), TILE)
            out = dot(pre[u, pl.ds(0, pair)], wd[:, column], ((1,), (0,))).astype(BF16)
            dx = (
                dot(pre[u, pl.ds(2 * pair, pair)], wg[column, :], ((1,), (1,)))
                + dot(pre[u, pl.ds(pair, pair)], wu[column, :], ((1,), (1,)))
            ).astype(BF16)
            lane = pl.ds(pl.multiple_of(n % per * TILE, TILE), TILE)
            for k, value in enumerate((out, dx)):
                low = pl.multiple_of((2 * k + n // per) * rows, rows)
                home = dot(back[:, :pair], value, ((1,), (0,))).astype(BF16)
                far[u, pl.ds(low, rows), lane] = home[:rows]
                sib_out[u % 2, pl.ds(low, rows), lane] = home[rows:]
            return 0

        lax.fori_loop(0, cols, emit, 0, unroll=4)
        start(part_copies(u))

    chunk = 64

    def combine(u, incoming):
        loads = [pltpu.make_async_copy(sib_in.at[u], tmp.at[0], load_sem.at[0])]
        wait_recv(part_copies(u))
        loads[0].start()
        totals = sm_acc[u] + sm_sib_in[u]
        for k, slot in enumerate(incoming):
            wait_recv(home_copies(u, slot, behind))
            loads.append(pltpu.make_async_copy(ring_in.at[slot], tmp.at[k + 1], load_sem.at[k + 1]))
            loads[-1].start()
            totals = totals + sm_ring_in[slot]
        for copy in loads:
            copy.wait()
        sm_acc[u] = totals

        def add(n, _):
            part = pl.ds(pl.multiple_of(n * chunk, chunk), chunk)
            total = far[u, part].astype(F32)
            for k in range(len(loads)):
                total = total + tmp[k, part].astype(F32)
            far[u, part] = total.astype(BF16)
            return 0

        lax.fori_loop(0, 4 * rows // chunk, add, 0)

    def send_home(u):
        if u == half:
            combine(u, [])
            start(home_copies(u, half - 1 + 2 * core, turn))
        elif u < half:
            if u == half - 1:
                pl.when(core == 0)(lambda: combine(u, [u]))
                pl.when(core == 1)(lambda: combine(u, []))
            else:
                combine(u, [u])
            start(home_copies(u, u - 1, ahead))
        else:
            if u == half + 1:
                pl.when(core == 1)(lambda: combine(u, [u]))
                pl.when(core == 0)(lambda: combine(u, []))
            else:
                combine(u, [u])
            start(home_copies(u, u + 1, behind))

    def gradient(k):
        target = (g_down, g_up, g_gate)[k]
        parts = width // hidden

        def whole(column):
            return pre[:, pl.ds(k * pair, pair), column].reshape(chips * pair, -1)

        def tile_of(n, size=TILE):
            return pl.ds(pl.multiple_of(n * size, size), size)

        def put(n):
            if k == 0:
                return target.at[tile_of(n // parts), tile_of(n % parts, hidden)]
            return target.at[tile_of(n)]

        def store(n, slot):
            return pltpu.make_async_copy(stage.at[slot], put(n), load_sem.at[2 + slot])

        def step(n, _):
            slot = n % 2
            if k == 0:
                left = whole(tile_of(n // parts))
                right = xc[:, pl.ds(pl.multiple_of(width + n % parts * hidden, hidden), hidden)]
            else:
                left, right = xc[:, tile_of(n)], whole(pl.ds(0, hidden))
            total = dot(left, right, ((0,), (0,)))
            pl.when(n >= 2)(lambda: store(n - 2, slot).wait())
            stage[slot] = total.astype(BF16)
            store(n, slot).start()
            return 0

        lax.fori_loop(0, cols, step, 0, unroll=2)
        for n in (cols - 2, cols - 1):
            store(n, n % 2).wait()

    def turn_of(i, _):
        for step in range(1, half + 1):
            pl.when(i == step)(functools.partial(forward, step))

        pl.when(i < chips)(lambda: project(i))
        for k in range(1, half):
            pl.when(i == half + 1 + k)(functools.partial(send_home, half - k))

        pl.when(i > 0)(lambda: respond(i - 1))
        for k in range(half):
            pl.when(i == half + 1 + k)(functools.partial(send_home, half + k))
        return 0

    lax.fori_loop(0, chips + 1, turn_of, 0)
    for k in range(3):
        gradient(k)

    combine(0, [0, chips])
    grad_gates[...] = sm_acc[0]
    for k, target in enumerate((mixed, grad_tokens)):
        for part in range(2):
            target[:, part * hidden:(part + 1) * hidden] = far[0, (2 * k + part) * rows:(2 * k + part + 1) * rows]

    for v in range(2, chips - 1):
        wait_send(ring_copies(v, v, behind))
    for u in range(chips):
        if u > 0:
            wait_send(side_copies(u))
        copies = part_copies(u)
        if u >= chips - 2:
            copies[0].wait_send()
        copies[1].wait_send()
    for slot in range(chips + 1):
        if slot not in (half - 1, half, half + 1):
            wait_send(home_copies(0, slot, behind))
    wait_send(home_copies(0, half - 1 + 2 * core, turn))


def ring_local(tokens, expert_ids, gates, cotangent, partner, w_gate, w_up, w_down):
    n_exp = lax.axis_size("expert")
    rows, width = tokens.shape
    hidden = w_gate.shape[2]
    top = expert_ids.shape[1]
    cap = rows * top // n_exp
    slots = cap + cap // 2
    chips = n_exp // 2
    pair = 2 * slots
    fits = width == 2 * hidden and hidden % TILE == 0 and slots % 16 == 0
    if not fits or rows != 128 or slots > rows or 4 * rows > 3 * pair or top % 8 or n_exp < 16:
        return local(tokens, expert_ids, gates, cotangent, partner, w_gate, w_up, w_down)
    small = jnp.concatenate([expert_ids.T.astype(F32), gates.T], axis=0)

    anywhere = pl.BlockSpec(memory_space=pl.ANY)
    inside = pl.BlockSpec(memory_space=pltpu.VMEM)
    shape = jax.ShapeDtypeStruct
    dma = pltpu.SemaphoreType.DMA
    vmem = pltpu.VMEM
    outs = pl.pallas_call(
        functools.partial(ring_kernel, n_exp, rows, top, cap, slots, width, hidden),
        out_shape=(
            shape((rows, width), BF16),
            shape((rows, width), BF16),
            shape((top, rows), F32),
            shape((width, hidden), BF16),
            shape((width, hidden), BF16),
            shape((hidden, width), BF16),
            shape((chips, rows, 2 * width), BF16),
            shape((chips, rows, 2 * width), BF16),
            shape((chips, 4 * rows, hidden), BF16),
            shape((chips + 1, 4 * rows, hidden), BF16),
        ),
        in_specs=[inside] * 2 + [anywhere] * 5,
        out_specs=(inside,) * 3 + (anywhere,) * 7,
        scratch_shapes=[
            vmem((width, hidden), BF16),
            vmem((width, hidden), BF16),
            vmem((hidden, width), BF16),
            vmem((2 * rows, 2 * width), BF16),
            vmem((chips * pair, 2 * width), BF16),
            vmem((chips, 3 * pair, hidden), BF16),
            vmem((chips, 3 * pair, hidden), BF16),
            vmem((2, 4 * rows, hidden), BF16),
            vmem((3, 4 * rows, hidden), BF16),
            vmem((2, TILE, hidden), BF16),
            vmem((chips, 2 * top, rows), F32),
            vmem((chips, 2 * top, rows), F32),
            vmem((chips, top, rows), F32),
            vmem((chips, top, rows), F32),
            vmem((chips, top, rows), F32),
            vmem((chips + 1, top, rows), F32),
            vmem((pair, 128), F32),
            vmem((pair, 128), F32),
            vmem((2 * rows, 2 * rows), BF16),
            vmem((pair, 2 * rows), BF16),
            dma((5,)),
        ] + [dma((chips,))] * 8 + [dma((3, chips))] * 2 + [dma((chips,))] * 4 + [dma((chips + 1,))] * 4,
        compiler_params=pltpu.CompilerParams(
            collective_id=0, has_side_effects=True, vmem_limit_bytes=60 * 1024 * 1024
        ),
        cost_estimate=pl.CostEstimate(
            flops=18 * chips * pair * width * hidden,
            bytes_accessed=12 * width * hidden,
            transcendentals=chips * pair * hidden,
        ),
    )(small, partner.reshape(1, -1), tokens, cotangent, w_gate[0], w_up[0], w_down[0])
    mixed, grad_tokens, grad_gates, g_gate, g_up, g_down = outs[:6]
    return mixed, grad_tokens, grad_gates.T, g_gate[None], g_up[None], g_down[None]


def local(tokens, expert_ids, gates, cotangent, partner, w_gate, w_up, w_down):
    n_exp = lax.axis_size("expert")
    n_dp = lax.axis_size("dp")
    me = lax.axis_index("expert")
    rows, width = tokens.shape
    top = expert_ids.shape[1]
    cap = rows * top // n_exp
    slots = cap + cap // 2
    own_gate, own_up, own_down = w_gate[0], w_up[0], w_down[0]

    small = jnp.concatenate([expert_ids.T.astype(jnp.float32), gates.T], axis=0)
    small = lax.all_gather(small, "expert", axis=0, tiled=False)
    all_x = lax.all_gather(tokens, "expert", axis=0, tiled=False)
    later, all_x = lax.optimization_barrier((cotangent, all_x))
    all_c = lax.all_gather(later, "expert", axis=0, tiled=False)

    hit = small[:, :top] == me.astype(jnp.float32)
    present = jnp.any(hit, axis=1)
    token_gate = jnp.sum(jnp.where(hit, small[:, top:], 0.0), axis=1)
    order = jnp.arange(rows)
    earlier = (order[:, None] < order[None, :]).astype(jnp.bfloat16)
    rank = dot(present.astype(jnp.bfloat16), earlier, ((1,), (0,))).astype(jnp.int32)
    limit = jnp.where(jnp.any(partner == me), slots, cap)
    taken = jnp.logical_and(present, rank < limit)
    place = jnp.where(taken, rank, -1)
    match = place[:, None, :] == jnp.arange(slots)[None, :, None]
    onehot = match.astype(jnp.bfloat16)
    slot_gate = jnp.sum(jnp.where(match, token_gate[:, None, :], 0.0), axis=2).reshape(-1, 1)
    back = (jnp.arange(slots)[None, None, :] == place[:, :, None]).astype(jnp.bfloat16)

    xs = rows_of(onehot, all_x)
    pre_g = dot(xs, own_gate, ((1,), (0,))).astype(jnp.bfloat16)
    pre_u = dot(xs, own_up, ((1,), (0,))).astype(jnp.bfloat16)
    cs = rows_of(onehot, all_c)
    pre_d = dot(cs, own_down, ((1,), (1,))).astype(jnp.bfloat16)

    if n_dp == 2:
        swap = [(0, 1), (1, 0)]

        def exchange(part):
            return (part, lax.ppermute(part, "dp", swap))

        def summed(both):
            return both[0].astype(jnp.float32) + both[1].astype(jnp.float32)

        def full(part):
            return part
    else:

        def exchange(part):
            return (lax.psum_scatter(part, "dp", scatter_dimension=1, tiled=True),)

        def summed(both):
            return both[0].astype(jnp.float32)

        def full(part):
            return lax.all_gather(part, "dp", axis=1, tiled=True)

    sum_g = exchange(pre_g)
    sum_u = exchange(pre_u)
    sum_d = exchange(pre_d)
    sum_g, sum_u, _ = lax.optimization_barrier((sum_g, sum_u, pre_d))
    gate_pre = summed(sum_g)
    up_pre = summed(sum_u)
    sig = jax.nn.sigmoid(gate_pre)
    act = gate_pre * sig
    hid = act * up_pre
    scaled_hid = full((slot_gate * hid).astype(jnp.bfloat16))

    def to_tokens(slot_rows):
        return rows_of(back, slot_rows.reshape(n_exp, slots, width))

    def send_home(parts):
        return lax.psum_scatter(parts, "expert", scatter_dimension=0, tiled=True)

    out = dot(scaled_hid, own_down, ((1,), (0,))).astype(jnp.bfloat16)
    out_parts = to_tokens(out)
    mixed = send_home(out_parts)

    sum_d, sum_g, sum_u, _ = lax.optimization_barrier((sum_d, sum_g, sum_u, out_parts))
    gate_pre = summed(sum_g)
    up_pre = summed(sum_u)
    sig = jax.nn.sigmoid(gate_pre)
    act = gate_pre * sig
    hid = act * up_pre
    raw = summed(sum_d)
    dhid = slot_gate * raw
    dup = full((dhid * act).astype(jnp.bfloat16))
    dgate = full((dhid * up_pre * sig * (1.0 + gate_pre * (1.0 - sig))).astype(jnp.bfloat16))
    slot_terms = jnp.sum(hid * raw, axis=1).reshape(n_exp, 1, slots)
    dx = (dot(dgate, own_gate, ((1,), (1,))) + dot(dup, own_up, ((1,), (1,)))).astype(jnp.bfloat16)
    grad_tokens = send_home(to_tokens(dx))

    mine = place[:, :, None] == jnp.arange(slots)[None, None, :]
    terms = jnp.sum(jnp.where(mine, slot_terms, 0.0), axis=2)
    terms = lax.all_to_all(terms, "expert", split_axis=0, concat_axis=0, tiled=True)
    labels = jnp.arange(n_exp, dtype=jnp.int32)
    chosen = expert_ids.T[None, :, :] == labels[:, None, None]
    grad_gates = jnp.sum(jnp.where(chosen, terms[:, None, :], 0.0), axis=0).T
    if n_dp != 2:
        grad_gates = lax.psum(grad_gates, "dp")

    grad_down = dot(scaled_hid, cs, ((0,), (0,))).astype(jnp.bfloat16)
    grad_up = dot(xs, dup, ((0,), (0,))).astype(jnp.bfloat16)
    grad_gate = dot(xs, dgate, ((0,), (0,))).astype(jnp.bfloat16)
    return (mixed, grad_tokens, grad_gates, grad_gate[None], grad_up[None], grad_down[None])


def solution(mesh):
    placed = (
        P("expert", "dp"),
        P("expert", None),
        P("expert", None),
        P("expert", "dp"),
        P(),
        P("expert", "dp", None),
        P("expert", "dp", None),
        P("expert", None, "dp"),
    )
    paired = mesh.shape["dp"] == 2 and mesh.shape["expert"] % 4 == 0
    return jax.shard_map(
        ring_local if paired else local,
        mesh=mesh,
        in_specs=placed,
        out_specs=(
            P("expert", "dp"),
            P("expert", "dp"),
            P("expert", None),
            P("expert", "dp", None),
            P("expert", "dp", None),
            P("expert", None, "dp"),
        ),
        check_vma=False,
    )
```

```python
import functools

import jax
import jax.numpy as jnp
from jax import lax
from jax.experimental import pallas as pl
from jax.experimental.pallas import tpu as pltpu
from jax.sharding import PartitionSpec as P

F32, BF16 = jnp.float32, jnp.bfloat16
MESH = pl.DeviceIdType.MESH
TILE = 256


def dot(left, right, dims):
    return lax.dot_general(left, right, (dims, ((), ())), preferred_element_type=jnp.float32)


def rows_of(onehot, values):
    rows = lax.dot_general(
        onehot, values, (((2,), (1,)), ((0,), (0,))), preferred_element_type=jnp.float32
    )
    return rows.astype(jnp.bfloat16).reshape(-1, values.shape[2])


def ring_kernel(
    n_exp, rows, top, cap, slots, width, hidden,
    small, partner, tokens, cot, w_gate, w_up, w_down,
    mixed, grad_tokens, grad_gates, g_gate, g_up, g_down, held, other, sib_in, ring_in,
    wg, wu, wd, blk, xc, pre, far, sib_out, tmp, stage,
    sm_held, sm_other, sm_acc, sm_sib_out, sm_sib_in, sm_ring_in,
    sgate, sacc, back, picks,
    grad_sem, load_sem, ag_s, ag_r, sg_s, sg_r, mag_s, mag_r, msg_s, msg_r,
    x_s, x_r, sp_s, sp_r, msp_s, msp_r, rp_s, rp_r, mrp_s, mrp_r,
):
    chips = n_exp // 2
    half = chips // 2
    pair = 2 * slots
    per = hidden // TILE
    cols = width // TILE

    dp = lax.axis_index("dp")
    me = lax.axis_index("expert")
    core = me % 2
    chip = me // 2
    y, z = chip % 2, chip // 2
    spot = z + y * (chips - 1 - 2 * z)

    def at_spot(q):
        q = q % chips
        hi = q // half
        return 2 * (2 * (q + hi * (chips - 1 - 2 * q)) + hi) + core

    ahead = (dp, at_spot(spot + chips + 1 - 2 * core))
    behind = (dp, at_spot(spot + chips - 1 + 2 * core))
    sibling = (dp, me + 1 - 2 * core)
    across = (1 - dp, me)

    def remote(src, dst, send, recv, to):
        return pltpu.make_async_remote_copy(
            src_ref=src, dst_ref=dst, send_sem=send, recv_sem=recv,
            device_id=to, device_id_type=MESH,
        )

    def ring_copies(src, dst, to, block=None):
        block = held.at[src] if block is None else block
        return (
            remote(block, held.at[dst], ag_s.at[dst], ag_r.at[dst], to),
            remote(sm_held.at[src], sm_held.at[dst], mag_s.at[dst], mag_r.at[dst], to),
        )

    def side_copies(u, block=None):
        block = held.at[u] if block is None else block
        return (
            remote(block, other.at[u], sg_s.at[u], sg_r.at[u], sibling),
            remote(sm_held.at[u], sm_other.at[u], msg_s.at[u], msg_r.at[u], sibling),
        )

    def x_copy(u, k):
        part = pl.ds(k * pair, pair)
        return remote(pre.at[u, part], far.at[u, part], x_s.at[k, u], x_r.at[k, u], across)

    def part_copies(u):
        return (
            remote(sib_out.at[u % 2], sib_in.at[u], sp_s.at[u], sp_r.at[u], sibling),
            remote(sm_sib_out.at[u], sm_sib_in.at[u], msp_s.at[u], msp_r.at[u], sibling),
        )

    def home_copies(u, dst, to):
        return (
            remote(far.at[u, pl.ds(0, 4 * rows)], ring_in.at[dst], rp_s.at[dst], rp_r.at[dst], to),
            remote(sm_acc.at[u], sm_ring_in.at[dst], mrp_s.at[dst], mrp_r.at[dst], to),
        )

    def start(copies):
        for copy in copies:
            copy.start()

    def wait_recv(copies):
        for copy in copies:
            copy.wait_recv()

    def wait_send(copies):
        for copy in copies:
            copy.wait_send()

    own = (
        pltpu.make_async_copy(tokens, blk.at[pl.ds(0, rows), pl.ds(0, width)], load_sem.at[0]),
        pltpu.make_async_copy(cot, blk.at[pl.ds(0, rows), pl.ds(width, width)], load_sem.at[1]),
    )
    weights = (
        pltpu.make_async_copy(w_gate, wg, load_sem.at[2]),
        pltpu.make_async_copy(w_up, wu, load_sem.at[3]),
        pltpu.make_async_copy(w_down, wd, load_sem.at[4]),
    )
    start(own)
    start(weights)
    sm_held[0] = small[...]

    barrier = pltpu.get_barrier_semaphore()
    for to in (ahead, behind, sibling, across):
        pl.semaphore_signal(barrier, inc=1, device_id=to, device_id_type=MESH)
    pl.semaphore_wait(barrier, 4)

    for copy in own:
        copy.wait()
    start(side_copies(0, blk.at[pl.ds(0, rows)]))
    start(ring_copies(0, 1, behind, blk.at[pl.ds(0, rows)]))
    start(ring_copies(0, chips - 1, ahead, blk.at[pl.ds(0, rows)]))

    me_f = me.astype(F32)
    hosted = jnp.max(jnp.where(partner[...] == me, 1.0, 0.0), axis=1, keepdims=True)
    limit = slots - (1.0 - hosted) * (slots - cap)

    def routes(info):
        ids, gates = info[:top], info[top:]
        hit = ids == me_f
        present = jnp.max(jnp.where(hit, 1.0, 0.0), axis=0, keepdims=True)
        gate = jnp.sum(jnp.where(hit, gates, 0.0), axis=0, keepdims=True)
        earlier = (
            lax.broadcasted_iota(jnp.int32, (rows, rows), 0)
            < lax.broadcasted_iota(jnp.int32, (rows, rows), 1)
        ).astype(F32).astype(BF16)
        spread = jnp.broadcast_to(present, (16, rows)).astype(BF16)
        rank = dot(spread, earlier, ((1,), (0,)))[:1]
        taken = jnp.where(rank < limit, present, 0.0)
        place = jnp.where(taken > 0.0, rank, -1.0)
        index = lax.broadcasted_iota(jnp.int32, (rows, rows), 0).astype(F32)
        match = jnp.where(index == place, 1.0, 0.0)
        return hit, gate, match

    def diagonal(matches):
        low = jnp.zeros((slots, rows), F32)
        left = jnp.concatenate([matches[0][:slots], low], axis=0)
        right = jnp.concatenate([low, matches[1][:slots]], axis=0)
        both = jnp.concatenate([left, right], axis=1)
        return jnp.concatenate([both, jnp.zeros((2 * (rows - slots), 2 * rows), F32)], axis=0)

    def info_of(u, b):
        return (sm_held, sm_other)[b][u]

    def forward(step):
        arrived = [step] if step == half else [step, chips - step]
        for v in arrived:
            wait_recv(ring_copies(v, v, behind))
        if step == 1:
            wait_send(side_copies(0) + ring_copies(0, 1, behind) + ring_copies(0, chips - 1, ahead))
        if step < half - 1:
            start(ring_copies(step, step + 1, behind))
            start(ring_copies(chips - step, chips - step - 1, ahead))
        elif step == half - 1:
            start(ring_copies(half + 1, half, ahead))
        for v in arrived:
            start(side_copies(v))

    def project(u):
        wait_recv(side_copies(u))
        loads = [
            pltpu.make_async_copy(source.at[u], blk.at[pl.ds(b * rows, rows)], load_sem.at[b])
            for b, source in enumerate((held, other))
        ]

        @pl.when(u > 0)
        def _():
            loads[0].start()

        loads[1].start()
        picks[...] = diagonal([routes(info_of(u, b))[2] for b in range(2)])[:pair].astype(BF16)
        pl.when(u > 0)(lambda: loads[0].wait())
        loads[1].wait()
        first = pl.multiple_of(u * pair, pair)

        def gather(n, _):
            column = pl.ds(pl.multiple_of(n * 2 * TILE, 2 * TILE), 2 * TILE)
            xc[pl.ds(first, pair), column] = dot(picks[...], blk[:, column], ((1,), (0,))).astype(BF16)
            return 0

        lax.fori_loop(0, cols, gather, 0, unroll=4)
        band = pl.ds(first, pair)

        for k in range(3):
            pl.when(u == 0)(lambda k=k: weights[k].wait())
            part = pl.ds(k * pair, pair)

            def product(n, _):
                column = pl.ds(pl.multiple_of(n * TILE, TILE), TILE)
                if k < 2:
                    got = dot(xc[band, pl.ds(0, width)], (wg, wu)[k][:, column], ((1,), (0,)))
                else:
                    got = dot(xc[band, pl.ds(width, width)], wd[column, :], ((1,), (1,)))
                pre[u, part, column] = got.astype(BF16)
                return 0

            lax.fori_loop(0, per, product, 0, unroll=4)
            x_copy(u, k).start()

    def respond(u):
        hits = []
        matches = []
        for b in range(2):
            hit, gate, match = routes(info_of(u, b))
            weight = jnp.sum(match * gate, axis=1, keepdims=True)
            sgate[pl.ds(b * slots, slots)] = jnp.broadcast_to(weight[:slots], (slots, 128))
            hits.append(hit)
            matches.append(match[:slots])
        back[...] = diagonal(matches).T.astype(BF16)
        sacc[...] = jnp.zeros_like(sacc)
        for k in range(3):
            x_copy(u, k).wait()

        def activate(n, _):
            column = pl.ds(pl.multiple_of(n * 128, 128), 128)

            def total(k):
                part = pl.ds(k * pair, pair)
                return pre[u, part, column].astype(F32) + far[u, part, column].astype(F32)

            gate_pre, up_pre, raw = total(0), total(1), total(2)
            sig = 1.0 / (1.0 + jnp.exp(-gate_pre))
            act = gate_pre * sig
            hid = act * up_pre
            scale = sgate[...]
            dhid = scale * raw
            sacc[...] += hid * raw
            pre[u, pl.ds(0, pair), column] = (scale * hid).astype(BF16)
            pre[u, pl.ds(pair, pair), column] = (dhid * act).astype(BF16)
            slope = sig * (1.0 + gate_pre * (1.0 - sig))
            pre[u, pl.ds(2 * pair, pair), column] = (dhid * up_pre * slope).astype(BF16)
            return 0

        lax.fori_loop(0, hidden // 128, activate, 0)

        for b in range(2):
            term = jnp.sum(sacc[pl.ds(b * slots, slots)], axis=1, keepdims=True)
            spread = jnp.sum(matches[b] * term, axis=0, keepdims=True)
            (sm_acc, sm_sib_out)[b][u] = jnp.where(hits[b], spread, 0.0)

        @pl.when(u >= 2)
        def _():
            part_copies(u - 2)[0].wait_send()

        def emit(n, _):
            column = pl.ds(pl.multiple_of(n * TILE, TILE), TILE)
            out = dot(pre[u, pl.ds(0, pair)], wd[:, column], ((1,), (0,))).astype(BF16)
            dx = (
                dot(pre[u, pl.ds(2 * pair, pair)], wg[column, :], ((1,), (1,)))
                + dot(pre[u, pl.ds(pair, pair)], wu[column, :], ((1,), (1,)))
            ).astype(BF16)
            lane = pl.ds(pl.multiple_of(n % per * TILE, TILE), TILE)
            for k, value in enumerate((out, dx)):
                low = pl.multiple_of((2 * k + n // per) * rows, rows)
                home = dot(back[:, :pair], value, ((1,), (0,))).astype(BF16)
                far[u, pl.ds(low, rows), lane] = home[:rows]
                sib_out[u % 2, pl.ds(low, rows), lane] = home[rows:]
            return 0

        lax.fori_loop(0, cols, emit, 0, unroll=4)
        start(part_copies(u))

    chunk = 64

    def combine(u, incoming):
        loads = [pltpu.make_async_copy(sib_in.at[u], tmp.at[0], load_sem.at[0])]
        wait_recv(part_copies(u))
        loads[0].start()
        totals = sm_acc[u] + sm_sib_in[u]
        for k, slot in enumerate(incoming):
            wait_recv(home_copies(u, slot, behind))
            loads.append(pltpu.make_async_copy(ring_in.at[slot], tmp.at[k + 1], load_sem.at[k + 1]))
            loads[-1].start()
            totals = totals + sm_ring_in[slot]
        for copy in loads:
            copy.wait()
        sm_acc[u] = totals

        def add(n, _):
            part = pl.ds(pl.multiple_of(n * chunk, chunk), chunk)
            total = far[u, part].astype(F32)
            for k in range(len(loads)):
                total = total + tmp[k, part].astype(F32)
            far[u, part] = total.astype(BF16)
            return 0

        lax.fori_loop(0, 4 * rows // chunk, add, 0)

    def send_home(u):
        if u == half:
            combine(u, [])
            start(home_copies(u, u - 1, ahead))
        elif u < half:
            if u == half - 1:
                combine(u, [u])
            else:
                combine(u, [u])
            start(home_copies(u, u - 1, ahead))
        else:
            if u == half + 1:
                combine(u, [])
            else:
                combine(u, [u])
            start(home_copies(u, u + 1, behind))

    def gradient(kinds):
        parts = width // hidden

        def whole(k, column):
            return pre[:, pl.ds(k * pair, pair), column].reshape(chips * pair, -1)

        def tile_of(n, size=TILE):
            return pl.ds(pl.multiple_of(n * size, size), size)

        def store(j, n, slot):
            k = kinds[j]
            if k == 0:
                target = g_down.at[tile_of(n // parts), tile_of(n % parts, hidden)]
            else:
                target = (g_up, g_gate)[k - 1].at[tile_of(n)]
            return pltpu.make_async_copy(stage.at[j, slot], target, grad_sem.at[j, slot])

        def step(n, _):
            slot = n % 2
            totals = []
            for k in kinds:
                if k == 0:
                    left = whole(0, tile_of(n // parts))
                    right = xc[:, pl.ds(pl.multiple_of(width + n % parts * hidden, hidden), hidden)]
                else:
                    left, right = xc[:, tile_of(n)], whole(k, pl.ds(0, hidden))
                totals.append(dot(left, right, ((0,), (0,))).astype(BF16))
            for j, total in enumerate(totals):
                pl.when(n >= 2)(lambda j=j: store(j, n - 2, slot).wait())
                stage[j, slot] = total
                store(j, n, slot).start()
            return 0

        lax.fori_loop(0, cols, step, 0, unroll=2)
        for n in (cols - 2, cols - 1):
            for j in range(len(kinds)):
                store(j, n, n % 2).wait()

    def turn_of(i, _):
        for step in range(1, half + 1):
            pl.when(i == step)(functools.partial(forward, step))

        pl.when(i < chips)(lambda: project(i))
        for k in range(1, half):
            pl.when(i == half + 1 + k)(functools.partial(send_home, half - k))

        pl.when(i > 0)(lambda: respond(i - 1))
        for k in range(half):
            pl.when(i == half + 1 + k)(functools.partial(send_home, half + k))
        return 0

    lax.fori_loop(0, chips + 1, turn_of, 0)
    gradient((2, 1))
    gradient((0,))

    combine(0, [0, chips])
    grad_gates[...] = sm_acc[0]
    for k, target in enumerate((mixed, grad_tokens)):
        for part in range(2):
            target[:, part * hidden:(part + 1) * hidden] = far[0, (2 * k + part) * rows:(2 * k + part + 1) * rows]

    for v in range(2, chips - 1):
        wait_send(ring_copies(v, v, behind))
    for u in range(chips):
        if u > 0:
            wait_send(side_copies(u))
        copies = part_copies(u)
        if u >= chips - 2:
            copies[0].wait_send()
        copies[1].wait_send()
    for slot in range(chips + 1):
        if slot not in (half, half + 1):
            wait_send(home_copies(0, slot, behind))


def ring_local(tokens, expert_ids, gates, cotangent, partner, w_gate, w_up, w_down):
    n_exp = lax.axis_size("expert")
    rows, width = tokens.shape
    hidden = w_gate.shape[2]
    top = expert_ids.shape[1]
    cap = rows * top // n_exp
    slots = cap + cap // 2
    chips = n_exp // 2
    pair = 2 * slots
    fits = width == 2 * hidden and hidden % TILE == 0 and slots % 16 == 0
    if not fits or rows != 128 or slots > rows or 4 * rows > 3 * pair or top % 8 or n_exp < 16:
        return local(tokens, expert_ids, gates, cotangent, partner, w_gate, w_up, w_down)
    small = jnp.concatenate([expert_ids.T.astype(F32), gates.T], axis=0)

    anywhere = pl.BlockSpec(memory_space=pl.ANY)
    inside = pl.BlockSpec(memory_space=pltpu.VMEM)
    shape = jax.ShapeDtypeStruct
    dma = pltpu.SemaphoreType.DMA
    vmem = pltpu.VMEM
    outs = pl.pallas_call(
        functools.partial(ring_kernel, n_exp, rows, top, cap, slots, width, hidden),
        out_shape=(
            shape((rows, width), BF16),
            shape((rows, width), BF16),
            shape((top, rows), F32),
            shape((width, hidden), BF16),
            shape((width, hidden), BF16),
            shape((hidden, width), BF16),
            shape((chips, rows, 2 * width), BF16),
            shape((chips, rows, 2 * width), BF16),
            shape((chips, 4 * rows, hidden), BF16),
            shape((chips + 1, 4 * rows, hidden), BF16),
        ),
        in_specs=[inside] * 2 + [anywhere] * 5,
        out_specs=(inside,) * 3 + (anywhere,) * 7,
        scratch_shapes=[
            vmem((width, hidden), BF16),
            vmem((width, hidden), BF16),
            vmem((hidden, width), BF16),
            vmem((2 * rows, 2 * width), BF16),
            vmem((chips * pair, 2 * width), BF16),
            vmem((chips, 3 * pair, hidden), BF16),
            vmem((chips, 3 * pair, hidden), BF16),
            vmem((2, 4 * rows, hidden), BF16),
            vmem((3, 4 * rows, hidden), BF16),
            vmem((2, 2, TILE, hidden), BF16),
            vmem((chips, 2 * top, rows), F32),
            vmem((chips, 2 * top, rows), F32),
            vmem((chips, top, rows), F32),
            vmem((chips, top, rows), F32),
            vmem((chips, top, rows), F32),
            vmem((chips + 1, top, rows), F32),
            vmem((pair, 128), F32),
            vmem((pair, 128), F32),
            vmem((2 * rows, 2 * rows), BF16),
            vmem((pair, 2 * rows), BF16),
            dma((2, 2)),
            dma((5,)),
        ] + [dma((chips,))] * 8 + [dma((3, chips))] * 2 + [dma((chips,))] * 4 + [dma((chips + 1,))] * 4,
        compiler_params=pltpu.CompilerParams(
            collective_id=0, has_side_effects=True, vmem_limit_bytes=60 * 1024 * 1024
        ),
        cost_estimate=pl.CostEstimate(
            flops=18 * chips * pair * width * hidden,
            bytes_accessed=12 * width * hidden,
            transcendentals=chips * pair * hidden,
        ),
    )(small, partner.reshape(1, -1), tokens, cotangent, w_gate[0], w_up[0], w_down[0])
    mixed, grad_tokens, grad_gates, g_gate, g_up, g_down = outs[:6]
    return mixed, grad_tokens, grad_gates.T, g_gate[None], g_up[None], g_down[None]


def local(tokens, expert_ids, gates, cotangent, partner, w_gate, w_up, w_down):
    n_exp = lax.axis_size("expert")
    n_dp = lax.axis_size("dp")
    me = lax.axis_index("expert")
    rows, width = tokens.shape
    top = expert_ids.shape[1]
    cap = rows * top // n_exp
    slots = cap + cap // 2
    own_gate, own_up, own_down = w_gate[0], w_up[0], w_down[0]

    small = jnp.concatenate([expert_ids.T.astype(jnp.float32), gates.T], axis=0)
    small = lax.all_gather(small, "expert", axis=0, tiled=False)
    all_x = lax.all_gather(tokens, "expert", axis=0, tiled=False)
    later, all_x = lax.optimization_barrier((cotangent, all_x))
    all_c = lax.all_gather(later, "expert", axis=0, tiled=False)

    hit = small[:, :top] == me.astype(jnp.float32)
    present = jnp.any(hit, axis=1)
    token_gate = jnp.sum(jnp.where(hit, small[:, top:], 0.0), axis=1)
    order = jnp.arange(rows)
    earlier = (order[:, None] < order[None, :]).astype(jnp.bfloat16)
    rank = dot(present.astype(jnp.bfloat16), earlier, ((1,), (0,))).astype(jnp.int32)
    limit = jnp.where(jnp.any(partner == me), slots, cap)
    taken = jnp.logical_and(present, rank < limit)
    place = jnp.where(taken, rank, -1)
    match = place[:, None, :] == jnp.arange(slots)[None, :, None]
    onehot = match.astype(jnp.bfloat16)
    slot_gate = jnp.sum(jnp.where(match, token_gate[:, None, :], 0.0), axis=2).reshape(-1, 1)
    back = (jnp.arange(slots)[None, None, :] == place[:, :, None]).astype(jnp.bfloat16)

    xs = rows_of(onehot, all_x)
    pre_g = dot(xs, own_gate, ((1,), (0,))).astype(jnp.bfloat16)
    pre_u = dot(xs, own_up, ((1,), (0,))).astype(jnp.bfloat16)
    cs = rows_of(onehot, all_c)
    pre_d = dot(cs, own_down, ((1,), (1,))).astype(jnp.bfloat16)

    if n_dp == 2:
        swap = [(0, 1), (1, 0)]

        def exchange(part):
            return (part, lax.ppermute(part, "dp", swap))

        def summed(both):
            return both[0].astype(jnp.float32) + both[1].astype(jnp.float32)

        def full(part):
            return part
    else:

        def exchange(part):
            return (lax.psum_scatter(part, "dp", scatter_dimension=1, tiled=True),)

        def summed(both):
            return both[0].astype(jnp.float32)

        def full(part):
            return lax.all_gather(part, "dp", axis=1, tiled=True)

    sum_g = exchange(pre_g)
    sum_u = exchange(pre_u)
    sum_d = exchange(pre_d)
    sum_g, sum_u, _ = lax.optimization_barrier((sum_g, sum_u, pre_d))
    gate_pre = summed(sum_g)
    up_pre = summed(sum_u)
    sig = jax.nn.sigmoid(gate_pre)
    act = gate_pre * sig
    hid = act * up_pre
    scaled_hid = full((slot_gate * hid).astype(jnp.bfloat16))

    def to_tokens(slot_rows):
        return rows_of(back, slot_rows.reshape(n_exp, slots, width))

    def send_home(parts):
        return lax.psum_scatter(parts, "expert", scatter_dimension=0, tiled=True)

    out = dot(scaled_hid, own_down, ((1,), (0,))).astype(jnp.bfloat16)
    out_parts = to_tokens(out)
    mixed = send_home(out_parts)

    sum_d, sum_g, sum_u, _ = lax.optimization_barrier((sum_d, sum_g, sum_u, out_parts))
    gate_pre = summed(sum_g)
    up_pre = summed(sum_u)
    sig = jax.nn.sigmoid(gate_pre)
    act = gate_pre * sig
    hid = act * up_pre
    raw = summed(sum_d)
    dhid = slot_gate * raw
    dup = full((dhid * act).astype(jnp.bfloat16))
    dgate = full((dhid * up_pre * sig * (1.0 + gate_pre * (1.0 - sig))).astype(jnp.bfloat16))
    slot_terms = jnp.sum(hid * raw, axis=1).reshape(n_exp, 1, slots)
    dx = (dot(dgate, own_gate, ((1,), (1,))) + dot(dup, own_up, ((1,), (1,)))).astype(jnp.bfloat16)
    grad_tokens = send_home(to_tokens(dx))

    mine = place[:, :, None] == jnp.arange(slots)[None, None, :]
    terms = jnp.sum(jnp.where(mine, slot_terms, 0.0), axis=2)
    terms = lax.all_to_all(terms, "expert", split_axis=0, concat_axis=0, tiled=True)
    labels = jnp.arange(n_exp, dtype=jnp.int32)
    chosen = expert_ids.T[None, :, :] == labels[:, None, None]
    grad_gates = jnp.sum(jnp.where(chosen, terms[:, None, :], 0.0), axis=0).T
    if n_dp != 2:
        grad_gates = lax.psum(grad_gates, "dp")

    grad_down = dot(scaled_hid, cs, ((0,), (0,))).astype(jnp.bfloat16)
    grad_up = dot(xs, dup, ((0,), (0,))).astype(jnp.bfloat16)
    grad_gate = dot(xs, dgate, ((0,), (0,))).astype(jnp.bfloat16)
    return (mixed, grad_tokens, grad_gates, grad_gate[None], grad_up[None], grad_down[None])


def solution(mesh):
    placed = (
        P("expert", "dp"),
        P("expert", None),
        P("expert", None),
        P("expert", "dp"),
        P(),
        P("expert", "dp", None),
        P("expert", "dp", None),
        P("expert", None, "dp"),
    )
    paired = mesh.shape["dp"] == 2 and mesh.shape["expert"] % 4 == 0
    return jax.shard_map(
        ring_local if paired else local,
        mesh=mesh,
        in_specs=placed,
        out_specs=(
            P("expert", "dp"),
            P("expert", "dp"),
            P("expert", None),
            P("expert", "dp", None),
            P("expert", "dp", None),
            P("expert", None, "dp"),
        ),
        check_vma=False,
    )
```

```python
import functools

import jax
import jax.numpy as jnp
from jax import lax
from jax.experimental import pallas as pl
from jax.experimental.pallas import tpu as pltpu
from jax.sharding import PartitionSpec as P

F32, BF16 = jnp.float32, jnp.bfloat16
MESH = pl.DeviceIdType.MESH
TILE = 256


def dot(left, right, dims):
    return lax.dot_general(left, right, (dims, ((), ())), preferred_element_type=jnp.float32)


def rows_of(onehot, values):
    rows = lax.dot_general(
        onehot, values, (((2,), (1,)), ((0,), (0,))), preferred_element_type=jnp.float32
    )
    return rows.astype(jnp.bfloat16).reshape(-1, values.shape[2])


def ring_kernel(
    n_exp, rows, top, cap, slots, width, hidden,
    small, partner, tokens, cot, w_gate, w_up, w_down,
    mixed, grad_tokens, grad_gates, g_gate, g_up, g_down, held, other, sib_in, ring_in,
    wg, wu, wd, blk, xc, pre, far, sib_out, tmp, stage,
    sm_held, sm_other, sm_acc, sm_sib_out, sm_sib_in, sm_ring_in,
    sgate, sacc, back, picks,
    grad_sem, load_sem, ag_s, ag_r, sg_s, sg_r, mag_s, mag_r, msg_s, msg_r,
    x_s, x_r, sp_s, sp_r, msp_s, msp_r, rp_s, rp_r, mrp_s, mrp_r,
):
    chips = n_exp // 2
    half = chips // 2
    pair = 2 * slots
    per = hidden // TILE
    cols = width // TILE

    dp = lax.axis_index("dp")
    me = lax.axis_index("expert")
    core = me % 2
    chip = me // 2
    y, z = chip % 2, chip // 2
    spot = z + y * (chips - 1 - 2 * z)

    def at_spot(q):
        q = q % chips
        hi = q // half
        return 2 * (2 * (q + hi * (chips - 1 - 2 * q)) + hi) + core

    ahead = (dp, at_spot(spot + chips + 1 - 2 * core))
    behind = (dp, at_spot(spot + chips - 1 + 2 * core))
    sibling = (dp, me + 1 - 2 * core)
    across = (1 - dp, me)

    def remote(src, dst, send, recv, to):
        return pltpu.make_async_remote_copy(
            src_ref=src, dst_ref=dst, send_sem=send, recv_sem=recv,
            device_id=to, device_id_type=MESH,
        )

    def ring_copies(src, dst, to, block=None):
        block = held.at[src] if block is None else block
        return (
            remote(block, held.at[dst], ag_s.at[dst], ag_r.at[dst], to),
            remote(sm_held.at[src], sm_held.at[dst], mag_s.at[dst], mag_r.at[dst], to),
        )

    def side_copies(u, block=None, target=None):
        block = held.at[u] if block is None else block
        target = other.at[u] if target is None else target
        return (
            remote(block, target, sg_s.at[u], sg_r.at[u], sibling),
            remote(sm_held.at[u], sm_other.at[u], msg_s.at[u], msg_r.at[u], sibling),
        )

    def x_copy(u, k):
        part = pl.ds(k * pair, pair)
        return remote(pre.at[u, part], far.at[u, part], x_s.at[k, u], x_r.at[k, u], across)

    def part_copies(u):
        return (
            remote(sib_out.at[u % 2], sib_in.at[u], sp_s.at[u], sp_r.at[u], sibling),
            remote(sm_sib_out.at[u], sm_sib_in.at[u], msp_s.at[u], msp_r.at[u], sibling),
        )

    def home_copies(u, dst, to):
        return (
            remote(far.at[u, pl.ds(0, 4 * rows)], ring_in.at[dst], rp_s.at[dst], rp_r.at[dst], to),
            remote(sm_acc.at[u], sm_ring_in.at[dst], mrp_s.at[dst], mrp_r.at[dst], to),
        )

    def start(copies):
        for copy in copies:
            copy.start()

    def wait_recv(copies):
        for copy in copies:
            copy.wait_recv()

    def wait_send(copies):
        for copy in copies:
            copy.wait_send()

    own = (
        pltpu.make_async_copy(tokens, blk.at[pl.ds(0, rows), pl.ds(0, width)], load_sem.at[0]),
        pltpu.make_async_copy(cot, blk.at[pl.ds(0, rows), pl.ds(width, width)], load_sem.at[1]),
    )
    weights = (
        pltpu.make_async_copy(w_gate, wg, load_sem.at[2]),
        pltpu.make_async_copy(w_up, wu, load_sem.at[3]),
        pltpu.make_async_copy(w_down, wd, load_sem.at[4]),
    )
    start(own)
    start(weights)
    sm_held[0] = small[...]

    barrier = pltpu.get_barrier_semaphore()
    for to in (ahead, behind, sibling, across):
        pl.semaphore_signal(barrier, inc=1, device_id=to, device_id_type=MESH)
    pl.semaphore_wait(barrier, 4)

    for copy in own:
        copy.wait()
    start(side_copies(0, blk.at[pl.ds(0, rows)], blk.at[pl.ds(rows, rows)]))
    start(ring_copies(0, 1, behind, blk.at[pl.ds(0, rows)]))
    start(ring_copies(0, chips - 1, ahead, blk.at[pl.ds(0, rows)]))

    me_f = me.astype(F32)
    hosted = jnp.max(jnp.where(partner[...] == me, 1.0, 0.0), axis=1, keepdims=True)
    limit = slots - (1.0 - hosted) * (slots - cap)

    def routes(info):
        ids, gates = info[:top], info[top:]
        hit = ids == me_f
        present = jnp.max(jnp.where(hit, 1.0, 0.0), axis=0, keepdims=True)
        gate = jnp.sum(jnp.where(hit, gates, 0.0), axis=0, keepdims=True)
        earlier = (
            lax.broadcasted_iota(jnp.int32, (rows, rows), 0)
            < lax.broadcasted_iota(jnp.int32, (rows, rows), 1)
        ).astype(F32).astype(BF16)
        spread = jnp.broadcast_to(present, (16, rows)).astype(BF16)
        rank = dot(spread, earlier, ((1,), (0,)))[:1]
        taken = jnp.where(rank < limit, present, 0.0)
        place = jnp.where(taken > 0.0, rank, -1.0)
        index = lax.broadcasted_iota(jnp.int32, (rows, rows), 0).astype(F32)
        match = jnp.where(index == place, 1.0, 0.0)
        return hit, gate, match

    def diagonal(matches):
        low = jnp.zeros((slots, rows), F32)
        left = jnp.concatenate([matches[0][:slots], low], axis=0)
        right = jnp.concatenate([low, matches[1][:slots]], axis=0)
        both = jnp.concatenate([left, right], axis=1)
        return jnp.concatenate([both, jnp.zeros((2 * (rows - slots), 2 * rows), F32)], axis=0)

    def info_of(u, b):
        return (sm_held, sm_other)[b][u]

    def forward(step):
        arrived = [step] if step == half else [step, chips - step]
        for v in arrived:
            wait_recv(ring_copies(v, v, behind))
        if step == 1:
            wait_send(side_copies(0) + ring_copies(0, 1, behind) + ring_copies(0, chips - 1, ahead))
        if step < half - 1:
            start(ring_copies(step, step + 1, behind))
            start(ring_copies(chips - step, chips - step - 1, ahead))
        elif step == half - 1:
            start(ring_copies(half + 1, half, ahead))
        for v in arrived:
            start(side_copies(v))

    def project(u):
        wait_recv(side_copies(u))
        loads = [
            pltpu.make_async_copy(source.at[u], blk.at[pl.ds(b * rows, rows)], load_sem.at[b])
            for b, source in enumerate((held, other))
        ]

        @pl.when(u > 0)
        def _():
            start(loads)

        picks[...] = diagonal([routes(info_of(u, b))[2] for b in range(2)])[:pair].astype(BF16)
        @pl.when(u > 0)
        def _():
            for copy in loads:
                copy.wait()

        first = pl.multiple_of(u * pair, pair)

        def gather(n, _):
            column = pl.ds(pl.multiple_of(n * 2 * TILE, 2 * TILE), 2 * TILE)
            xc[pl.ds(first, pair), column] = dot(picks[...], blk[:, column], ((1,), (0,))).astype(BF16)
            return 0

        lax.fori_loop(0, cols, gather, 0, unroll=4)
        band = pl.ds(first, pair)

        for k in range(3):
            pl.when(u == 0)(lambda k=k: weights[k].wait())
            part = pl.ds(k * pair, pair)

            def product(n, _):
                column = pl.ds(pl.multiple_of(n * TILE, TILE), TILE)
                if k < 2:
                    got = dot(xc[band, pl.ds(0, width)], (wg, wu)[k][:, column], ((1,), (0,)))
                else:
                    got = dot(xc[band, pl.ds(width, width)], wd[column, :], ((1,), (1,)))
                pre[u, part, column] = got.astype(BF16)
                return 0

            lax.fori_loop(0, per, product, 0, unroll=4)
            x_copy(u, k).start()

    def respond(u):
        hits = []
        matches = []
        for b in range(2):
            hit, gate, match = routes(info_of(u, b))
            weight = jnp.sum(match * gate, axis=1, keepdims=True)
            sgate[pl.ds(b * slots, slots)] = jnp.broadcast_to(weight[:slots], (slots, 128))
            hits.append(hit)
            matches.append(match[:slots])
        back[...] = diagonal(matches).T.astype(BF16)
        sacc[...] = jnp.zeros_like(sacc)
        for k in range(3):
            x_copy(u, k).wait()

        def activate(n, _):
            column = pl.ds(pl.multiple_of(n * 128, 128), 128)

            def total(k):
                part = pl.ds(k * pair, pair)
                return pre[u, part, column].astype(F32) + far[u, part, column].astype(F32)

            gate_pre, up_pre, raw = total(0), total(1), total(2)
            sig = 1.0 / (1.0 + jnp.exp(-gate_pre))
            act = gate_pre * sig
            hid = act * up_pre
            scale = sgate[...]
            dhid = scale * raw
            sacc[...] += hid * raw
            pre[u, pl.ds(0, pair), column] = (scale * hid).astype(BF16)
            pre[u, pl.ds(pair, pair), column] = (dhid * act).astype(BF16)
            slope = sig * (1.0 + gate_pre * (1.0 - sig))
            pre[u, pl.ds(2 * pair, pair), column] = (dhid * up_pre * slope).astype(BF16)
            return 0

        lax.fori_loop(0, hidden // 128, activate, 0)

        for b in range(2):
            term = jnp.sum(sacc[pl.ds(b * slots, slots)], axis=1, keepdims=True)
            spread = jnp.sum(matches[b] * term, axis=0, keepdims=True)
            (sm_acc, sm_sib_out)[b][u] = jnp.where(hits[b], spread, 0.0)

        @pl.when(u >= 2)
        def _():
            part_copies(u - 2)[0].wait_send()

        def emit(n, _):
            column = pl.ds(pl.multiple_of(n * TILE, TILE), TILE)
            out = dot(pre[u, pl.ds(0, pair)], wd[:, column], ((1,), (0,))).astype(BF16)
            dx = (
                dot(pre[u, pl.ds(2 * pair, pair)], wg[column, :], ((1,), (1,)))
                + dot(pre[u, pl.ds(pair, pair)], wu[column, :], ((1,), (1,)))
            ).astype(BF16)
            lane = pl.ds(pl.multiple_of(n % per * TILE, TILE), TILE)
            for k, value in enumerate((out, dx)):
                low = pl.multiple_of((2 * k + n // per) * rows, rows)
                home = dot(back[:, :pair], value, ((1,), (0,))).astype(BF16)
                far[u, pl.ds(low, rows), lane] = home[:rows]
                sib_out[u % 2, pl.ds(low, rows), lane] = home[rows:]
            return 0

        lax.fori_loop(0, cols, emit, 0, unroll=4)
        start(part_copies(u))

    chunk = 64

    def combine(u, incoming):
        loads = []
        for k, slot in enumerate(incoming):
            wait_recv(home_copies(u, slot, behind))
            loads.append(pltpu.make_async_copy(ring_in.at[slot], tmp.at[k + 1], load_sem.at[k + 1]))
            loads[-1].start()
        wait_recv(part_copies(u))
        loads.append(pltpu.make_async_copy(sib_in.at[u], tmp.at[0], load_sem.at[0]))
        loads[-1].start()
        totals = sm_acc[u] + sm_sib_in[u]
        for slot in incoming:
            totals = totals + sm_ring_in[slot]
        for copy in loads:
            copy.wait()
        sm_acc[u] = totals

        def add(n, _):
            part = pl.ds(pl.multiple_of(n * chunk, chunk), chunk)
            total = far[u, part].astype(F32)
            for k in range(len(loads)):
                total = total + tmp[k, part].astype(F32)
            far[u, part] = total.astype(BF16)
            return 0

        lax.fori_loop(0, 4 * rows // chunk, add, 0)

    def send_home(u):
        if u == half:
            combine(u, [])
            start(home_copies(u, u - 1, ahead))
        elif u < half:
            if u == half - 1:
                combine(u, [u])
            else:
                combine(u, [u])
            start(home_copies(u, u - 1, ahead))
        else:
            if u == half + 1:
                combine(u, [])
            else:
                combine(u, [u])
            start(home_copies(u, u + 1, behind))

    def gradient(kinds):
        parts = width // hidden

        def whole(k, column):
            return pre[:, pl.ds(k * pair, pair), column].reshape(chips * pair, -1)

        def tile_of(n, size=TILE):
            return pl.ds(pl.multiple_of(n * size, size), size)

        def store(j, n, slot):
            k = kinds[j]
            if k == 0:
                target = g_down.at[tile_of(n // parts), tile_of(n % parts, hidden)]
            else:
                target = (g_up, g_gate)[k - 1].at[tile_of(n)]
            return pltpu.make_async_copy(stage.at[j, slot], target, grad_sem.at[j, slot])

        def step(n, _):
            slot = n % 2
            totals = []
            for k in kinds:
                if k == 0:
                    left = whole(0, tile_of(n // parts))
                    right = xc[:, pl.ds(pl.multiple_of(width + n % parts * hidden, hidden), hidden)]
                else:
                    left, right = xc[:, tile_of(n)], whole(k, pl.ds(0, hidden))
                totals.append(dot(left, right, ((0,), (0,))).astype(BF16))
            for j, total in enumerate(totals):
                pl.when(n >= 2)(lambda j=j: store(j, n - 2, slot).wait())
                stage[j, slot] = total
                store(j, n, slot).start()
            return 0

        lax.fori_loop(0, cols, step, 0, unroll=2)
        for n in (cols - 2, cols - 1):
            for j in range(len(kinds)):
                store(j, n, n % 2).wait()

    def turn_of(i, _):
        for step in range(1, half + 1):
            pl.when(i == step)(functools.partial(forward, step))

        pl.when(i < chips)(lambda: project(i))
        for k in range(1, half):
            pl.when(i == half + 1 + k)(functools.partial(send_home, half - k))

        pl.when(i > 0)(lambda: respond(i - 1))
        for k in range(half):
            pl.when(i == half + 1 + k)(functools.partial(send_home, half + k))
        return 0

    lax.fori_loop(0, chips + 1, turn_of, 0)
    gradient((2, 1))
    gradient((0,))

    combine(0, [0, chips])
    grad_gates[...] = sm_acc[0]
    for k, target in enumerate((mixed, grad_tokens)):
        for part in range(2):
            target[:, part * hidden:(part + 1) * hidden] = far[0, (2 * k + part) * rows:(2 * k + part + 1) * rows]

    for v in range(2, chips - 1):
        wait_send(ring_copies(v, v, behind))
    for u in range(chips):
        if u > 0:
            wait_send(side_copies(u))
        copies = part_copies(u)
        if u >= chips - 2:
            copies[0].wait_send()
        copies[1].wait_send()
    for slot in range(chips + 1):
        if slot not in (half, half + 1):
            wait_send(home_copies(0, slot, behind))


def ring_local(tokens, expert_ids, gates, cotangent, partner, w_gate, w_up, w_down):
    n_exp = lax.axis_size("expert")
    rows, width = tokens.shape
    hidden = w_gate.shape[2]
    top = expert_ids.shape[1]
    cap = rows * top // n_exp
    slots = cap + cap // 2
    chips = n_exp // 2
    pair = 2 * slots
    fits = width == 2 * hidden and hidden % TILE == 0 and slots % 16 == 0
    if not fits or rows != 128 or slots > rows or 4 * rows > 3 * pair or top % 8 or n_exp < 16:
        return local(tokens, expert_ids, gates, cotangent, partner, w_gate, w_up, w_down)
    small = jnp.concatenate([expert_ids.T.astype(F32), gates.T], axis=0)

    anywhere = pl.BlockSpec(memory_space=pl.ANY)
    inside = pl.BlockSpec(memory_space=pltpu.VMEM)
    shape = jax.ShapeDtypeStruct
    dma = pltpu.SemaphoreType.DMA
    vmem = pltpu.VMEM
    outs = pl.pallas_call(
        functools.partial(ring_kernel, n_exp, rows, top, cap, slots, width, hidden),
        out_shape=(
            shape((rows, width), BF16),
            shape((rows, width), BF16),
            shape((top, rows), F32),
            shape((width, hidden), BF16),
            shape((width, hidden), BF16),
            shape((hidden, width), BF16),
            shape((chips, rows, 2 * width), BF16),
            shape((chips, rows, 2 * width), BF16),
            shape((chips, 4 * rows, hidden), BF16),
            shape((chips + 1, 4 * rows, hidden), BF16),
        ),
        in_specs=[inside] * 2 + [anywhere] * 5,
        out_specs=(inside,) * 3 + (anywhere,) * 7,
        scratch_shapes=[
            vmem((width, hidden), BF16),
            vmem((width, hidden), BF16),
            vmem((hidden, width), BF16),
            vmem((2 * rows, 2 * width), BF16),
            vmem((chips * pair, 2 * width), BF16),
            vmem((chips, 3 * pair, hidden), BF16),
            vmem((chips, 3 * pair, hidden), BF16),
            vmem((2, 4 * rows, hidden), BF16),
            vmem((3, 4 * rows, hidden), BF16),
            vmem((2, 2, TILE, hidden), BF16),
            vmem((chips, 2 * top, rows), F32),
            vmem((chips, 2 * top, rows), F32),
            vmem((chips, top, rows), F32),
            vmem((chips, top, rows), F32),
            vmem((chips, top, rows), F32),
            vmem((chips + 1, top, rows), F32),
            vmem((pair, 128), F32),
            vmem((pair, 128), F32),
            vmem((2 * rows, 2 * rows), BF16),
            vmem((pair, 2 * rows), BF16),
            dma((2, 2)),
            dma((5,)),
        ] + [dma((chips,))] * 8 + [dma((3, chips))] * 2 + [dma((chips,))] * 4 + [dma((chips + 1,))] * 4,
        compiler_params=pltpu.CompilerParams(
            collective_id=0, has_side_effects=True, vmem_limit_bytes=60 * 1024 * 1024
        ),
        cost_estimate=pl.CostEstimate(
            flops=18 * chips * pair * width * hidden,
            bytes_accessed=12 * width * hidden,
            transcendentals=chips * pair * hidden,
        ),
    )(small, partner.reshape(1, -1), tokens, cotangent, w_gate[0], w_up[0], w_down[0])
    mixed, grad_tokens, grad_gates, g_gate, g_up, g_down = outs[:6]
    return mixed, grad_tokens, grad_gates.T, g_gate[None], g_up[None], g_down[None]


def local(tokens, expert_ids, gates, cotangent, partner, w_gate, w_up, w_down):
    n_exp = lax.axis_size("expert")
    n_dp = lax.axis_size("dp")
    me = lax.axis_index("expert")
    rows, width = tokens.shape
    top = expert_ids.shape[1]
    cap = rows * top // n_exp
    slots = cap + cap // 2
    own_gate, own_up, own_down = w_gate[0], w_up[0], w_down[0]

    small = jnp.concatenate([expert_ids.T.astype(jnp.float32), gates.T], axis=0)
    small = lax.all_gather(small, "expert", axis=0, tiled=False)
    all_x = lax.all_gather(tokens, "expert", axis=0, tiled=False)
    later, all_x = lax.optimization_barrier((cotangent, all_x))
    all_c = lax.all_gather(later, "expert", axis=0, tiled=False)

    hit = small[:, :top] == me.astype(jnp.float32)
    present = jnp.any(hit, axis=1)
    token_gate = jnp.sum(jnp.where(hit, small[:, top:], 0.0), axis=1)
    order = jnp.arange(rows)
    earlier = (order[:, None] < order[None, :]).astype(jnp.bfloat16)
    rank = dot(present.astype(jnp.bfloat16), earlier, ((1,), (0,))).astype(jnp.int32)
    limit = jnp.where(jnp.any(partner == me), slots, cap)
    taken = jnp.logical_and(present, rank < limit)
    place = jnp.where(taken, rank, -1)
    match = place[:, None, :] == jnp.arange(slots)[None, :, None]
    onehot = match.astype(jnp.bfloat16)
    slot_gate = jnp.sum(jnp.where(match, token_gate[:, None, :], 0.0), axis=2).reshape(-1, 1)
    back = (jnp.arange(slots)[None, None, :] == place[:, :, None]).astype(jnp.bfloat16)

    xs = rows_of(onehot, all_x)
    pre_g = dot(xs, own_gate, ((1,), (0,))).astype(jnp.bfloat16)
    pre_u = dot(xs, own_up, ((1,), (0,))).astype(jnp.bfloat16)
    cs = rows_of(onehot, all_c)
    pre_d = dot(cs, own_down, ((1,), (1,))).astype(jnp.bfloat16)

    if n_dp == 2:
        swap = [(0, 1), (1, 0)]

        def exchange(part):
            return (part, lax.ppermute(part, "dp", swap))

        def summed(both):
            return both[0].astype(jnp.float32) + both[1].astype(jnp.float32)

        def full(part):
            return part
    else:

        def exchange(part):
            return (lax.psum_scatter(part, "dp", scatter_dimension=1, tiled=True),)

        def summed(both):
            return both[0].astype(jnp.float32)

        def full(part):
            return lax.all_gather(part, "dp", axis=1, tiled=True)

    sum_g = exchange(pre_g)
    sum_u = exchange(pre_u)
    sum_d = exchange(pre_d)
    sum_g, sum_u, _ = lax.optimization_barrier((sum_g, sum_u, pre_d))
    gate_pre = summed(sum_g)
    up_pre = summed(sum_u)
    sig = jax.nn.sigmoid(gate_pre)
    act = gate_pre * sig
    hid = act * up_pre
    scaled_hid = full((slot_gate * hid).astype(jnp.bfloat16))

    def to_tokens(slot_rows):
        return rows_of(back, slot_rows.reshape(n_exp, slots, width))

    def send_home(parts):
        return lax.psum_scatter(parts, "expert", scatter_dimension=0, tiled=True)

    out = dot(scaled_hid, own_down, ((1,), (0,))).astype(jnp.bfloat16)
    out_parts = to_tokens(out)
    mixed = send_home(out_parts)

    sum_d, sum_g, sum_u, _ = lax.optimization_barrier((sum_d, sum_g, sum_u, out_parts))
    gate_pre = summed(sum_g)
    up_pre = summed(sum_u)
    sig = jax.nn.sigmoid(gate_pre)
    act = gate_pre * sig
    hid = act * up_pre
    raw = summed(sum_d)
    dhid = slot_gate * raw
    dup = full((dhid * act).astype(jnp.bfloat16))
    dgate = full((dhid * up_pre * sig * (1.0 + gate_pre * (1.0 - sig))).astype(jnp.bfloat16))
    slot_terms = jnp.sum(hid * raw, axis=1).reshape(n_exp, 1, slots)
    dx = (dot(dgate, own_gate, ((1,), (1,))) + dot(dup, own_up, ((1,), (1,)))).astype(jnp.bfloat16)
    grad_tokens = send_home(to_tokens(dx))

    mine = place[:, :, None] == jnp.arange(slots)[None, None, :]
    terms = jnp.sum(jnp.where(mine, slot_terms, 0.0), axis=2)
    terms = lax.all_to_all(terms, "expert", split_axis=0, concat_axis=0, tiled=True)
    labels = jnp.arange(n_exp, dtype=jnp.int32)
    chosen = expert_ids.T[None, :, :] == labels[:, None, None]
    grad_gates = jnp.sum(jnp.where(chosen, terms[:, None, :], 0.0), axis=0).T
    if n_dp != 2:
        grad_gates = lax.psum(grad_gates, "dp")

    grad_down = dot(scaled_hid, cs, ((0,), (0,))).astype(jnp.bfloat16)
    grad_up = dot(xs, dup, ((0,), (0,))).astype(jnp.bfloat16)
    grad_gate = dot(xs, dgate, ((0,), (0,))).astype(jnp.bfloat16)
    return (mixed, grad_tokens, grad_gates, grad_gate[None], grad_up[None], grad_down[None])


def solution(mesh):
    placed = (
        P("expert", "dp"),
        P("expert", None),
        P("expert", None),
        P("expert", "dp"),
        P(),
        P("expert", "dp", None),
        P("expert", "dp", None),
        P("expert", None, "dp"),
    )
    paired = mesh.shape["dp"] == 2 and mesh.shape["expert"] % 4 == 0
    return jax.shard_map(
        ring_local if paired else local,
        mesh=mesh,
        in_specs=placed,
        out_specs=(
            P("expert", "dp"),
            P("expert", "dp"),
            P("expert", None),
            P("expert", "dp", None),
            P("expert", "dp", None),
            P("expert", None, "dp"),
        ),
        check_vma=False,
    )
```
